512 devices in a mesh: dp: 64 (over x, y, z_hi, core), shard: 8 (over z_lo).
Axes of the slice: x: 4, y: 4, z: 16 (z_hi: 2, z_lo: 8; z = z_hi * 8 + z_lo), core: 2. Of those that a mesh axis runs over, the one named last changes fastest.
Arguments:
- group_grads: bfloat16 [64, 1024, 1024], P('dp', 'shard'), may hold values from -2 to 2
- moment: float32 [1024, 1024], P('shard'), may hold values from -6 to 6
- second: float32 [1024, 1024], P(None, 'shard'), may hold values from 0.5 to 4
- stat_left: float32 [1024, 1024], P('shard'), may hold values from -200 to 2000, as said below
- stat_right: float32 [1024, 1024], P('shard'), may hold values from -200 to 2000, as said below
- basis_left: float32 [1024, 1024], P('shard'), as said below
- basis_right: float32 [1024, 1024], P('shard'), as said below
Outputs:
- update: bfloat16 [1024, 1024], P('shard')
- second_new: float32 [1024, 1024], P(None, 'shard')
- left_new: float32 [1024, 1024], P('shard')
- right_new: float32 [1024, 1024], P('shard')
The draws below stay inside these ranges and needn't reach their ends.
Inputs may be any that keep to these rules, and one draw needn't show every extreme that they name: `stat_left`: each statistic is symmetric. `stat_right`: each statistic is symmetric. `basis_left`: diagonal entries near 0.9 sqrt(1024), off-diagonal entries of order one. `basis_right`: diagonal entries near 0.9 sqrt(1024), off-diagonal entries of order one.
All inputs are finite; a program needn't handle non-finite values.
Results may differ from the reference program's by a relative error of at most 0.0049.
The reference program's roundings to bfloat16 on the way count: a program that leaves them out, or rounds other values in their place, can miss the bound.
Values may be sent and summed in bfloat16 or wider, within the bound.
A program may use at most 128 MiB of HBM per device.

```python
import math
import jax
import jax.numpy as jnp
from jax import lax

B = 1024
NS_ITERS = 2
N_DP = 64


def statistic_draw(key):
    key_noise, key_rough = jax.random.split(key, 2)
    position = jnp.arange(B).astype(jnp.float32)
    noise = jnp.clip(jax.random.normal(key_noise, (B, B), jnp.float32), -3.0, 3.0)
    rough = jax.random.uniform(key_rough, (B,), jnp.float32, -0.35, 0.35)
    ramp = 1.0 + 3.0 * position / B
    symmetric = (noise + noise.T) * (0.35 / math.sqrt(B))
    scales = jnp.sqrt(ramp) * jnp.exp(rough)
    identity = (position[:, None] == position[None, :]).astype(jnp.float32)
    return 100.0 * scales[:, None] * scales[None, :] * (identity + symmetric)


def basis_draw(key):
    position = jnp.arange(B).astype(jnp.float32)
    noise = jnp.clip(0.45 * jax.random.normal(key, (B, B), jnp.float32), -2.5, 2.5)
    identity = (position[:, None] == position[None, :]).astype(jnp.float32)
    return 0.9 * math.sqrt(B) * identity + noise


def draw_stat_left(key, part):
    return statistic_draw(jax.random.fold_in(key, 11))


def draw_stat_right(key, part):
    return statistic_draw(jax.random.fold_in(key, 12))


def draw_basis_left(key, part):
    return basis_draw(jax.random.fold_in(key, 21))


def draw_basis_right(key, part):
    return basis_draw(jax.random.fold_in(key, 22))


def spiked(drawn, own_key, source, target, shards_of, factor):
    owner, partner = [(jnp.arange(drawn.shape[dim]) // (drawn.shape[dim] // shards_of)).reshape([-1 if axis == dim else 1 for axis in range(drawn.ndim)]) for dim in (source, target)]
    chosen = jax.random.permutation(own_key, shards_of)[partner]
    strong = (owner == chosen) | (owner == (partner + shards_of // 2) % shards_of)
    return jnp.where(strong, factor * drawn, drawn)


def levels(key, extent, cuts, low, largest):
    factor_of, own = 1.0, jax.random.fold_in(key, 6)
    for axis_at, blocks in cuts:
        steps = jnp.exp(jax.random.uniform(jax.random.fold_in(own, axis_at), (blocks,), jnp.float32, low / len(cuts), largest / len(cuts)))
        factor_of = factor_of * jnp.repeat(steps, extent[axis_at] // blocks).reshape([-1 if axis == axis_at else 1 for axis in range(len(extent))])
    return factor_of


def centred(own_key, extent, deviation, reach, cuts=(), dtype=jnp.bfloat16):
    entries = jax.random.normal(own_key, extent, jnp.float32) * deviation
    if len(cuts) > 0:
        entries = levels(own_key, extent, cuts, -0.22, 0.18) * entries
    return jnp.clip(entries, min=-reach, max=reach).astype(dtype)


def gaussian_with(stream_key, extent, width, most, cuts, heavy, held_as=jnp.bfloat16):
    entries = width * jax.random.normal(stream_key, extent, jnp.float32)
    if cuts:
        entries = entries * levels(stream_key, extent, cuts, -0.22, 0.18)
    return jnp.clip(spiked(entries, jax.random.fold_in(stream_key, 3), *heavy), -most, most).astype(held_as)


def setup_inputs(seed: int = 0) -> dict:
    key_list = jax.random.split(jax.random.key(seed), 8)
    return {
        "group_grads": gaussian_with(key_list[0], (N_DP, B, B), N_DP ** -0.5, 2.0, ((0, 64), (1, 8)), (0, 2, 64, 4.0)),
        "moment": centred(key_list[1], (B, B), 1.0, 6.0, ((0, 8),), jnp.float32),
        "second": jnp.clip(jnp.exp(math.log(4.0) - 2.0794415 * jax.random.uniform(key_list[2], (B, B), jnp.float32) ** levels(key_list[2], (B, B), ((1, 8),), -0.2, 0.2)), 0.5, 4.0),
        "stat_left": draw_stat_left(jax.random.fold_in(key_list[7], 71), 0),
        "stat_right": draw_stat_right(jax.random.fold_in(key_list[7], 71), 0),
        "basis_left": draw_basis_left(jax.random.fold_in(key_list[7], 71), 0),
        "basis_right": draw_basis_right(jax.random.fold_in(key_list[7], 71), 0),
    }


BETA_ONE = 0.9
BETA_TWO = 0.9
BETA_STAT = 0.95
EPSILON = 1e-08
NORM_EPS = 1e-06

def orthogonalize(statistic, basis_half):
    product = jnp.dot(statistic.astype(jnp.bfloat16), basis_half, preferred_element_type=jnp.float32)
    scaled = product / jnp.sqrt(lax.optimization_barrier(jnp.mean(product * product, axis=0)) + NORM_EPS)
    current = scaled.astype(jnp.bfloat16)
    result = scaled
    for iteration in range(NS_ITERS):
        gram = (jnp.dot(current, current.T, preferred_element_type=jnp.float32) / B).astype(jnp.bfloat16)
        result = 1.5 * current.astype(jnp.float32) - 0.5 * jnp.dot(gram, current, preferred_element_type=jnp.float32)
        if iteration + 1 < NS_ITERS:
            current = result.astype(jnp.bfloat16)
    return result

def reference(group_grads, moment, second, stat_left, stat_right, basis_left, basis_right):
    summed = lax.optimization_barrier(jnp.sum(group_grads.astype(jnp.float32), axis=0))
    gradient = summed.astype(jnp.bfloat16)
    moment_half = (BETA_ONE * moment + (1.0 - BETA_ONE) * gradient.astype(jnp.float32)).astype(jnp.bfloat16)
    left_stat = BETA_STAT * stat_left + (1.0 - BETA_STAT) * jnp.dot(gradient, gradient.T, preferred_element_type=jnp.float32)
    right_stat = BETA_STAT * stat_right + (1.0 - BETA_STAT) * jnp.dot(gradient.T, gradient, preferred_element_type=jnp.float32)
    left_rot = basis_left.astype(jnp.bfloat16)
    right_rot = basis_right.astype(jnp.bfloat16)
    grad_turned = jnp.dot(gradient, right_rot, preferred_element_type=jnp.float32).astype(jnp.bfloat16)
    moment_turned = jnp.dot(moment_half, right_rot, preferred_element_type=jnp.float32).astype(jnp.bfloat16)
    grad_rot = jnp.dot(left_rot.T, grad_turned, preferred_element_type=jnp.float32) / B
    moment_rot = jnp.dot(left_rot.T, moment_turned, preferred_element_type=jnp.float32) / B
    second_new = BETA_TWO * second + (1.0 - BETA_TWO) * grad_rot * grad_rot
    scaled = (moment_rot / (jnp.sqrt(second_new) + EPSILON)).astype(jnp.bfloat16)
    turned_back = jnp.dot(left_rot, scaled, preferred_element_type=jnp.float32).astype(jnp.bfloat16)
    update = (jnp.dot(turned_back, right_rot.T, preferred_element_type=jnp.float32) / B).astype(jnp.bfloat16)
    left_new = orthogonalize(left_stat, left_rot)
    right_new = orthogonalize(right_stat, right_rot)
    return (update, second_new, left_new, right_new)
```

```python
import jax
import jax.numpy as jnp
from jax import lax
from jax.experimental import pallas as pl
from jax.experimental.pallas import tpu as pltpu
from jax.sharding import PartitionSpec as P

NS_ITERS = 2


BETA_ONE = 0.9
BETA_TWO = 0.9
BETA_STAT = 0.95
EPSILON = 1e-08
NORM_EPS = 1e-06

ORDER = 1024
SHARDS = 8
ROWS = ORDER // SHARDS
SIDE = 4
COLS = ORDER // SIDE
COPIES = 100
LOCALS = 5


def contract_rows(left_mat, right_mat):
    return lax.dot_general(
        left_mat, right_mat, (((0,), (0,)), ((), ())), preferred_element_type=jnp.float32
    )


def contract_cols(left_mat, right_mat):
    return lax.dot_general(
        left_mat, right_mat, (((1,), (1,)), ((), ())), preferred_element_type=jnp.float32
    )


class Place:
    def __init__(self):
        data = lax.axis_index("dp")
        self.z = lax.axis_index("shard")
        self.core = lax.rem(data, 2)
        self.zhi = lax.rem(lax.div(data, 2), 2)
        y = lax.rem(lax.div(data, 4), 4)
        x = lax.div(data, 16)
        self.p = x + self.core * (y - x)
        self.q = y + self.core * (x - y)

    def at(self, p, q, zhi, core):
        x = p + self.core * (q - p)
        y = q + self.core * (p - q)
        return ((x * 4 + y) * 2 + zhi) * 2 + core

    def along_p(self, step):
        p = lax.rem(self.p + step, SIDE)
        return (self.at(p, self.q, self.zhi, self.core), self.z)

    def along_q(self, step):
        q = lax.rem(self.q + step, SIDE)
        return (self.at(self.p, q, self.zhi, self.core), self.z)

    def along_z(self, step):
        z = lax.rem(self.z + step, SHARDS)
        return (self.at(self.p, self.q, self.zhi, self.core), z)

    def far(self):
        return (self.at(self.p, self.q, 1 - self.zhi, self.core), self.z)

    def sibling(self):
        return (self.at(self.p, self.q, self.zhi, 1 - self.core), self.z)


class Copies:
    def __init__(self, send, recv):
        self.send, self.recv, self.count, self.started = send, recv, 0, []

    def start(self, src, dst, device):
        copy = pltpu.make_async_remote_copy(
            src_ref=src,
            dst_ref=dst,
            send_sem=self.send.at[self.count],
            recv_sem=self.recv.at[self.count],
            device_id=device,
            device_id_type=pl.DeviceIdType.MESH,
        )
        self.count += 1
        copy.start()
        self.started.append(copy)
        return copy

    def finish(self):
        for copy in self.started:
            copy.wait_send()


class Gather:
    def __init__(self, place, copies, local_sem, out, both):
        self.place, self.copies, self.local_sem = place, copies, local_sem
        self.out, self.both = out, both
        self.height = ROWS // SIDE // (2 if both else 1)
        self.base = place.core * (ROWS // 2) if both else 0
        self.to_core = []

    def rows(self, p):
        return pl.ds(pl.multiple_of(self.base + p * self.height, self.height), self.height)

    def cols(self, q):
        return pl.ds(pl.multiple_of(q * COLS, COLS), COLS)

    def piece(self, ref):
        return ref.at[self.rows(self.place.p), self.cols(self.place.q)]

    def z_stage(self, piece):
        place = self.place
        spot = self.out.at[place.z, self.rows(place.p), self.cols(place.q)]
        self.local = pltpu.make_async_copy(piece, spot, self.local_sem)
        self.local.start()
        self.stage = [
            self.copies.start(piece, spot, place.along_z(step)) for step in (7, 1, 6, 2, 5, 3, 4)
        ]

    def arrived(self):
        for copy in self.stage:
            copy.wait_recv()

    def q_spot(self, step, zs):
        q = lax.rem(self.place.q + step, SIDE)
        return self.out.at[zs, self.rows(self.place.p), self.cols(q)]

    def p_spot(self, step, zs):
        p = lax.rem(self.place.p + step, SIDE)
        return self.out.at[zs, self.rows(p), :]

    def q_first(self):
        self.local.wait()
        self.arrived()
        self.ring_first(self.q_spot, self.place.along_q)

    def q_second(self):
        self.arrived()
        self.ring_second(self.q_spot, self.place.along_q)

    def p_first(self):
        self.arrived()
        self.ring_first(self.p_spot, self.place.along_p)
        self.share(0)

    def p_second(self):
        self.arrived()
        self.ring_second(self.p_spot, self.place.along_p)
        self.share(1)
        self.share(3)

    def p_third(self):
        self.arrived()
        self.share(2)

    def finish(self):
        for copy in self.to_core:
            copy.wait_recv()

    def ring_first(self, spot, along):
        whole = pl.ds(0, SHARDS)
        own = spot(0, whole)
        self.stage = [
            self.copies.start(own, own, along(1)),
            self.copies.start(own, own, along(3)),
        ]

    def ring_second(self, spot, along):
        low, high = pl.ds(0, SHARDS // 2), pl.ds(SHARDS // 2, SHARDS // 2)
        self.stage = [
            self.copies.start(spot(3, low), spot(3, low), along(1)),
            self.copies.start(spot(1, high), spot(1, high), along(3)),
        ]

    def share(self, step):
        if self.both:
            block = self.p_spot(step, pl.ds(0, SHARDS))
            self.to_core.append(self.copies.start(block, block, self.place.sibling()))


def collect_kernel(
    grads, moment, stat, base_left, base_right,
    out_grad, out_moment, out_left, out_right, out_stat,
    recv0, acc0, recv1, acc1, recv2, acc2, recv3, grad_piece, moment_piece,
    send, recv, local,
):
    place = Place()
    barrier = pltpu.get_barrier_semaphore()
    partners = [place.sibling(), place.far()]
    partners += [place.along_p(step) for step in (1, 2, 3)]
    partners += [place.along_q(step) for step in (1, 2, 3)]
    partners += [place.along_z(step) for step in range(1, SHARDS)]
    for partner in partners:
        pl.semaphore_signal(
            barrier, inc=1, device_id=partner, device_id_type=pl.DeviceIdType.MESH
        )
    pl.semaphore_wait(barrier, len(partners))

    copies = Copies(send, recv)
    half = ROWS // 2
    mine = pl.ds(pl.multiple_of(place.core * half, half), half)
    theirs = pl.ds(pl.multiple_of((1 - place.core) * half, half), half)
    g, m, l, r, s = [
        Gather(place, copies, local.at[index], out, both)
        for index, (out, both) in enumerate(
            (
                (out_grad, True),
                (out_moment, True),
                (out_left, True),
                (out_right, True),
                (out_stat, False),
            )
        )
    ]

    core_copy = copies.start(grads.at[theirs, :], recv0, place.sibling())
    l.z_stage(l.piece(base_left))
    r.z_stage(r.piece(base_right))
    s.z_stage(s.piece(stat))

    core_copy.wait_recv()
    acc0[...] = (
        grads[mine, :].astype(jnp.float32) + recv0[...].astype(jnp.float32)
    ).reshape(acc0.shape)
    p_copies = [
        copies.start(
            acc0.at[lax.rem(place.p + step, SIDE)], recv1.at[step - 1], place.along_p(step)
        )
        for step in (1, 3, 2)
    ]
    for copy in p_copies:
        copy.wait_recv()
    acc1[...] = (acc0[place.p] + recv1[0]) + (recv1[1] + recv1[2])
    q_copies = [
        copies.start(
            acc1.at[:, g.cols(lax.rem(place.q + step, SIDE))],
            recv2.at[step - 1],
            place.along_q(step),
        )
        for step in (1, 3, 2)
    ]
    for copy in q_copies:
        copy.wait_recv()
    acc2[...] = (acc1[:, g.cols(place.q)] + recv2[0]) + (recv2[1] + recv2[2])
    far_copy = copies.start(acc2, recv3, place.far())
    l.q_first()
    r.q_first()
    far_copy.wait_recv()
    piece = (acc2[...] + recv3[...]).astype(jnp.bfloat16)
    grad_piece[...] = piece
    old = moment[g.rows(place.p), g.cols(place.q)]
    moment_piece[...] = (
        BETA_ONE * old + (1.0 - BETA_ONE) * piece.astype(jnp.float32)
    ).astype(jnp.bfloat16)
    g.z_stage(grad_piece)
    m.z_stage(moment_piece)

    l.q_second()
    r.q_second()
    s.q_first()
    l.p_first()
    r.p_first()
    s.q_second()
    g.q_first()
    m.q_first()
    s.p_first()
    g.q_second()
    m.q_second()
    l.p_second()
    r.p_second()
    g.p_first()
    m.p_first()
    l.p_third()
    r.p_third()
    s.p_second()
    g.p_second()
    m.p_second()
    g.p_third()
    m.p_third()
    s.p_third()
    for gather in (l, r, g, m):
        gather.finish()
    copies.finish()


def collect(grads, moment, stat, base_left, base_right):
    whole = (SHARDS, ROWS, ORDER)
    vmem = pl.BlockSpec(memory_space=pltpu.VMEM)
    outs = [jax.ShapeDtypeStruct(whole, jnp.bfloat16)] * 4
    outs += [jax.ShapeDtypeStruct(whole, jnp.float32)]
    height = ROWS // SIDE // 2
    f32, bf16 = jnp.float32, jnp.bfloat16
    return pl.pallas_call(
        collect_kernel,
        out_shape=outs,
        in_specs=[vmem] * 5,
        out_specs=[vmem] * 5,
        scratch_shapes=[
            pltpu.VMEM((ROWS // 2, ORDER), bf16),
            pltpu.VMEM((SIDE, height, ORDER), f32),
            pltpu.VMEM((SIDE - 1, height, ORDER), f32),
            pltpu.VMEM((height, ORDER), f32),
            pltpu.VMEM((SIDE - 1, height, COLS), f32),
            pltpu.VMEM((height, COLS), f32),
            pltpu.VMEM((height, COLS), f32),
            pltpu.VMEM((height, COLS), bf16),
            pltpu.VMEM((height, COLS), bf16),
            pltpu.SemaphoreType.DMA((COPIES,)),
            pltpu.SemaphoreType.DMA((COPIES,)),
            pltpu.SemaphoreType.DMA((LOCALS,)),
        ],
        compiler_params=pltpu.CompilerParams(collective_id=0, has_side_effects=True),
        name="collect",
    )(grads, moment, stat, base_left, base_right)


def body(group_grads, moment, second, stat_left, stat_right, basis_left, basis_right):
    position = lax.axis_index("shard")
    core = lax.rem(lax.axis_index("dp"), 2)
    is_left = core == 0
    row_start = position * ROWS
    gradient, moment_half, left_rot, right_rot, stat = collect(
        group_grads[0],
        moment,
        jnp.where(is_left, stat_left, stat_right),
        basis_left.astype(jnp.bfloat16),
        basis_right.astype(jnp.bfloat16),
    )
    gradient, moment_half, left_rot, right_rot, stat = [
        array.reshape(ORDER, ORDER)
        for array in (gradient, moment_half, left_rot, right_rot, stat)
    ]

    right_cols = lax.dynamic_slice_in_dim(right_rot, row_start, ROWS, 1)
    grad_block = jnp.dot(gradient, right_cols, preferred_element_type=jnp.float32).astype(
        jnp.bfloat16
    )
    moment_block = jnp.dot(moment_half, right_cols, preferred_element_type=jnp.float32).astype(
        jnp.bfloat16
    )
    grad_rot = contract_rows(left_rot, grad_block) / ORDER
    moment_rot = contract_rows(left_rot, moment_block) / ORDER
    second_new = BETA_TWO * second + (1.0 - BETA_TWO) * grad_rot * grad_rot
    scaled = (moment_rot / (jnp.sqrt(second_new) + EPSILON)).astype(jnp.bfloat16)
    turned_back = jnp.dot(left_rot, scaled, preferred_element_type=jnp.float32).astype(jnp.bfloat16)
    back_rows = lax.all_to_all(turned_back, "shard", split_axis=0, concat_axis=1, tiled=True)
    update = (contract_cols(back_rows, right_rot) / ORDER).astype(jnp.bfloat16)

    outer = lax.cond(
        is_left,
        lambda g: contract_cols(g, g),
        lambda g: contract_rows(g, g),
        gradient,
    )
    stat_new = (BETA_STAT * stat + (1.0 - BETA_STAT) * outer).astype(jnp.bfloat16)
    rot = jnp.where(is_left, left_rot, right_rot)
    product = jnp.dot(stat_new, rot, preferred_element_type=jnp.float32)
    squares = jnp.sum(product * product, axis=0)
    current = (product / jnp.sqrt(squares / ORDER + NORM_EPS)).astype(jnp.bfloat16)
    for _ in range(NS_ITERS - 1):
        gram = (contract_cols(current, current) / ORDER).astype(jnp.bfloat16)
        current = (
            1.5 * current.astype(jnp.float32)
            - 0.5 * jnp.dot(gram, current, preferred_element_type=jnp.float32)
        ).astype(jnp.bfloat16)
    rows = lax.dynamic_slice_in_dim(current, row_start, ROWS, 0)
    gram = (contract_cols(rows, current) / ORDER).astype(jnp.bfloat16)
    result = 1.5 * rows.astype(jnp.float32) - 0.5 * jnp.dot(
        gram, current, preferred_element_type=jnp.float32
    )
    size = lax.axis_size("dp")
    other = lax.ppermute(result, "dp", [(i, i ^ 1) for i in range(size)])
    left_result = jnp.where(is_left, result, other)
    right_result = jnp.where(is_left, other, result)
    return (update, second_new, left_result, right_result)


def solution(mesh):
    return jax.shard_map(
        body,
        mesh=mesh,
        in_specs=(
            P("dp", "shard", None),
            P("shard", None),
            P(None, "shard"),
            P("shard", None),
            P("shard", None),
            P("shard", None),
            P("shard", None),
        ),
        out_specs=(P("shard", None), P(None, "shard"), P("shard", None), P("shard", None)),
        check_vma=False,
    )
```

```python
import jax
import jax.numpy as jnp
from jax import lax
from jax.experimental import pallas as pl
from jax.experimental.pallas import tpu as pltpu
from jax.sharding import PartitionSpec as P

NS_ITERS = 2


BETA_ONE = 0.9
BETA_TWO = 0.9
BETA_STAT = 0.95
EPSILON = 1e-08
NORM_EPS = 1e-06

ORDER = 1024
SHARDS = 8
ROWS = ORDER // SHARDS
SIDE = 4
COLS = ORDER // SIDE
COPIES = 100
LOCALS = 6


def contract_rows(left_mat, right_mat):
    return lax.dot_general(
        left_mat, right_mat, (((0,), (0,)), ((), ())), preferred_element_type=jnp.float32
    )


def contract_cols(left_mat, right_mat):
    return lax.dot_general(
        left_mat, right_mat, (((1,), (1,)), ((), ())), preferred_element_type=jnp.float32
    )


class Place:
    def __init__(self):
        data = lax.axis_index("dp")
        self.z = lax.axis_index("shard")
        self.core = lax.rem(data, 2)
        self.zhi = lax.rem(lax.div(data, 2), 2)
        y = lax.rem(lax.div(data, 4), 4)
        x = lax.div(data, 16)
        self.p = x + self.core * (y - x)
        self.q = y + self.core * (x - y)

    def at(self, p, q, zhi, core):
        x = p + self.core * (q - p)
        y = q + self.core * (p - q)
        return ((x * 4 + y) * 2 + zhi) * 2 + core

    def along_p(self, step):
        p = lax.rem(self.p + step, SIDE)
        return (self.at(p, self.q, self.zhi, self.core), self.z)

    def along_q(self, step):
        q = lax.rem(self.q + step, SIDE)
        return (self.at(self.p, q, self.zhi, self.core), self.z)

    def along_z(self, step):
        z = lax.rem(self.z + step, SHARDS)
        return (self.at(self.p, self.q, self.zhi, self.core), z)

    def far(self):
        return (self.at(self.p, self.q, 1 - self.zhi, self.core), self.z)

    def sibling(self):
        return (self.at(self.p, self.q, self.zhi, 1 - self.core), self.z)


class Copies:
    def __init__(self, send, recv):
        self.send, self.recv, self.count, self.started = send, recv, 0, []

    def start(self, src, dst, device):
        copy = pltpu.make_async_remote_copy(
            src_ref=src,
            dst_ref=dst,
            send_sem=self.send.at[self.count],
            recv_sem=self.recv.at[self.count],
            device_id=device,
            device_id_type=pl.DeviceIdType.MESH,
        )
        self.count += 1
        copy.start()
        self.started.append(copy)
        return copy

    def finish(self):
        for copy in self.started:
            copy.wait_send()


class Ring:
    def __init__(self, copies, spot, along):
        self.copies, self.spot, self.along = copies, spot, along

    def first(self):
        own = self.spot(0, pl.ds(0, SHARDS))
        self.stage = [
            self.copies.start(own, own, self.along(1)),
            self.copies.start(own, own, self.along(3)),
        ]

    def second(self):
        self.arrived()
        low, high = pl.ds(0, SHARDS // 2), pl.ds(SHARDS // 2, SHARDS // 2)
        self.stage = [
            self.copies.start(self.spot(3, low), self.spot(3, low), self.along(1)),
            self.copies.start(self.spot(1, high), self.spot(1, high), self.along(3)),
        ]

    def arrived(self):
        for copy in self.stage:
            copy.wait_recv()


class Spread:
    def __init__(self, place, copies, piece, spot, local_sem):
        self.local = pltpu.make_async_copy(piece, spot, local_sem)
        self.local.start()
        self.stage = [
            copies.start(piece, spot, place.along_z(step)) for step in (7, 1, 6, 2, 5, 3, 4)
        ]

    def arrived(self):
        self.local.wait()
        for copy in self.stage:
            copy.wait_recv()


class Gather:
    def __init__(self, place, copies, local_sem, out):
        self.place, self.copies, self.local_sem, self.out = place, copies, local_sem, out
        self.q_ring = Ring(copies, self.q_spot, place.along_q)
        self.p_ring = Ring(copies, self.p_spot, place.along_p)
        self.to_core = []

    def rows(self, p):
        height = ROWS // SIDE // 2
        start = self.place.core * (ROWS // 2) + p * height
        return pl.ds(pl.multiple_of(start, height), height)

    def piece(self, ref):
        return ref.at[self.rows(self.place.p), cols(self.place.q)]

    def z_stage(self, piece):
        place = self.place
        spot = self.out.at[place.z, self.rows(place.p), cols(place.q)]
        self.spread = Spread(place, self.copies, piece, spot, self.local_sem)

    def q_spot(self, step, zs):
        q = lax.rem(self.place.q + step, SIDE)
        return self.out.at[zs, self.rows(self.place.p), cols(q)]

    def p_spot(self, step, zs):
        p = lax.rem(self.place.p + step, SIDE)
        return self.out.at[zs, self.rows(p), :]

    def q_first(self):
        self.spread.arrived()
        self.q_ring.first()

    def q_second(self):
        self.q_ring.second()

    def q_third(self):
        self.q_ring.arrived()

    def p_first(self):
        self.p_ring.first()
        self.share(0)

    def p_second(self):
        self.p_ring.second()
        self.share(1)
        self.share(3)

    def p_third(self):
        self.p_ring.arrived()
        self.share(2)

    def finish(self):
        for copy in self.to_core:
            copy.wait_recv()

    def share(self, step):
        block = self.p_spot(step, pl.ds(0, SHARDS))
        self.to_core.append(self.copies.start(block, block, self.place.sibling()))


def cols(q):
    return pl.ds(pl.multiple_of(q * COLS, COLS), COLS)


def renew_stat(place, grad, stat, out):
    mine = cols(place.q)

    def keep(pair, outer):
        new = BETA_STAT * stat[pair] + (1.0 - BETA_STAT) * outer.reshape(2, ROWS, COLS)
        out[pair, :, mine] = new.astype(jnp.bfloat16)

    @pl.when(place.core == 0)
    def _():
        other = grad[pl.ds(2 * place.q, 2)].reshape(COLS, ORDER)

        @pl.loop(0, SHARDS // 2)
        def _(index):
            pair = pl.ds(2 * index, 2)
            keep(pair, contract_cols(grad[pair].reshape(COLS, ORDER), other))

    @pl.when(place.core == 1)
    def _():
        other = grad[:, :, mine].reshape(ORDER, COLS)

        @pl.loop(0, SHARDS // 2)
        def _(index):
            block = grad[:, :, cols(index)].reshape(ORDER, COLS)
            keep(pl.ds(2 * index, 2), contract_rows(block, other))


def collect_kernel(
    grads, moment, stat, base_left, base_right,
    out_left, out_right, out_turned, out_stat,
    all_grad, all_moment, all_stat,
    recv0, acc0, recv1, acc1, recv2, acc2, recv3, grad_piece, moment_piece,
    send, recv, local,
):
    place = Place()
    barrier = pltpu.get_barrier_semaphore()
    partners = [place.sibling(), place.far()]
    partners += [place.along_p(step) for step in (1, 2, 3)]
    partners += [place.along_q(step) for step in (1, 2, 3)]
    partners += [place.along_z(step) for step in range(1, SHARDS)]
    for partner in partners:
        pl.semaphore_signal(
            barrier, inc=1, device_id=partner, device_id_type=pl.DeviceIdType.MESH
        )
    pl.semaphore_wait(barrier, len(partners))

    copies = Copies(send, recv)
    half = ROWS // 2
    mine = pl.ds(pl.multiple_of(place.core * half, half), half)
    theirs = pl.ds(pl.multiple_of((1 - place.core) * half, half), half)
    g, m, l, r, t = [
        Gather(place, copies, local.at[index], out)
        for index, out in enumerate((all_grad, all_moment, out_left, out_right, out_turned))
    ]

    def quarter(p):
        return pl.ds(pl.multiple_of(p * (ROWS // SIDE), ROWS // SIDE), ROWS // SIDE)

    def stat_p_spot(step, zs):
        return all_stat.at[zs, quarter(lax.rem(place.p + step, SIDE)), :]

    def stat_q_spot(step, zs):
        return out_stat.at[zs, :, cols(lax.rem(place.q + step, SIDE))]

    s_in = Ring(copies, stat_p_spot, place.along_p)
    s_out = Ring(copies, stat_q_spot, place.along_q)

    core_copy = copies.start(grads.at[theirs, :], recv0, place.sibling())
    l.z_stage(l.piece(base_left))
    r.z_stage(r.piece(base_right))
    s_spread = Spread(
        place,
        copies,
        stat.at[quarter(place.p), cols(place.q)],
        all_stat.at[place.z, quarter(place.p), :],
        local.at[5],
    )

    core_copy.wait_recv()
    acc0[...] = (
        grads[mine, :].astype(jnp.float32) + recv0[...].astype(jnp.float32)
    ).reshape(acc0.shape)
    p_copies = [
        copies.start(
            acc0.at[lax.rem(place.p + step, SIDE)], recv1.at[step - 1], place.along_p(step)
        )
        for step in (1, 3, 2)
    ]
    for copy in p_copies:
        copy.wait_recv()
    acc1[...] = (acc0[place.p] + recv1[0]) + (recv1[1] + recv1[2])
    q_copies = [
        copies.start(
            acc1.at[:, cols(lax.rem(place.q + step, SIDE))],
            recv2.at[step - 1],
            place.along_q(step),
        )
        for step in (1, 3, 2)
    ]
    for copy in q_copies:
        copy.wait_recv()
    acc2[...] = (acc1[:, cols(place.q)] + recv2[0]) + (recv2[1] + recv2[2])
    far_copy = copies.start(acc2, recv3, place.far())
    l.q_first()
    r.q_first()
    far_copy.wait_recv()
    piece = (acc2[...] + recv3[...]).astype(jnp.bfloat16)
    grad_piece[...] = piece
    old = moment[g.rows(place.p), cols(place.q)]
    moment_piece[...] = (
        BETA_ONE * old + (1.0 - BETA_ONE) * piece.astype(jnp.float32)
    ).astype(jnp.bfloat16)
    g.z_stage(grad_piece)
    m.z_stage(moment_piece)

    l.q_second()
    r.q_second()
    l.q_third()
    l.p_first()
    r.q_third()
    r.p_first()
    s_spread.arrived()
    s_in.first()
    g.q_first()
    m.q_first()
    r.p_second()
    l.p_second()
    s_in.second()
    g.q_second()
    m.q_second()
    r.p_third()
    l.p_third()
    g.q_third()
    g.p_first()
    m.q_third()
    r.finish()
    own = g.rows(place.p)
    height = ROWS // SIDE // 2
    pair = jnp.concatenate(
        [all_grad[:, own, :].reshape(ROWS, ORDER), all_moment[:, own, :].reshape(ROWS, ORDER)]
    )
    right_cols = out_right[:, :, pl.ds(pl.multiple_of(place.z * ROWS, ROWS), ROWS)]
    turned = jnp.dot(
        pair, right_cols.reshape(ORDER, ROWS), preferred_element_type=jnp.float32
    ).astype(jnp.bfloat16)
    out_turned[:, own, :ROWS] = turned[:ROWS].reshape(SHARDS, height, ROWS)
    out_turned[:, own, ROWS:] = turned[ROWS:].reshape(SHARDS, height, ROWS)
    g.p_second()
    t.p_first()
    g.p_third()
    t.p_second()
    s_in.arrived()
    g.finish()
    renew_stat(place, all_grad, all_stat, out_stat)
    s_out.first()
    t.p_third()
    s_out.second()
    s_out.arrived()
    l.finish()
    t.finish()
    copies.finish()


def collect(grads, moment, stat, base_left, base_right):
    whole = (SHARDS, ROWS, ORDER)
    part = (SHARDS, ROWS, COLS)
    vmem = pl.BlockSpec(memory_space=pltpu.VMEM)
    outs = [jax.ShapeDtypeStruct(shape, jnp.bfloat16) for shape in (whole, whole, part, whole)]
    height = ROWS // SIDE // 2
    f32, bf16 = jnp.float32, jnp.bfloat16
    return pl.pallas_call(
        collect_kernel,
        out_shape=outs,
        in_specs=[vmem] * 5,
        out_specs=[vmem] * 4,
        scratch_shapes=[
            pltpu.VMEM(whole, bf16),
            pltpu.VMEM(whole, bf16),
            pltpu.VMEM(part, f32),
            pltpu.VMEM((ROWS // 2, ORDER), bf16),
            pltpu.VMEM((SIDE, height, ORDER), f32),
            pltpu.VMEM((SIDE - 1, height, ORDER), f32),
            pltpu.VMEM((height, ORDER), f32),
            pltpu.VMEM((SIDE - 1, height, COLS), f32),
            pltpu.VMEM((height, COLS), f32),
            pltpu.VMEM((height, COLS), f32),
            pltpu.VMEM((height, COLS), bf16),
            pltpu.VMEM((height, COLS), bf16),
            pltpu.SemaphoreType.DMA((COPIES,)),
            pltpu.SemaphoreType.DMA((COPIES,)),
            pltpu.SemaphoreType.DMA((LOCALS,)),
        ],
        compiler_params=pltpu.CompilerParams(collective_id=0, has_side_effects=True),
        name="collect",
    )(grads, moment, stat, base_left, base_right)


def body(group_grads, moment, second, stat_left, stat_right, basis_left, basis_right):
    position = lax.axis_index("shard")
    core = lax.rem(lax.axis_index("dp"), 2)
    is_left = core == 0
    row_start = position * ROWS
    left_rot, right_rot, turned, stat_new = collect(
        group_grads[0],
        moment,
        jnp.where(is_left, stat_left, stat_right),
        basis_left.astype(jnp.bfloat16),
        basis_right.astype(jnp.bfloat16),
    )
    left_rot, right_rot, turned, stat_new = [
        array.reshape(ORDER, -1) for array in (left_rot, right_rot, turned, stat_new)
    ]

    rotated = contract_rows(left_rot, turned) / ORDER
    grad_rot, moment_rot = rotated[:, :ROWS], rotated[:, ROWS:]
    second_new = BETA_TWO * second + (1.0 - BETA_TWO) * grad_rot * grad_rot
    scaled = (moment_rot / (jnp.sqrt(second_new) + EPSILON)).astype(jnp.bfloat16)
    turned_back = jnp.dot(left_rot, scaled, preferred_element_type=jnp.float32).astype(jnp.bfloat16)
    back_rows = lax.all_to_all(turned_back, "shard", split_axis=0, concat_axis=1, tiled=True)
    update = (contract_cols(back_rows, right_rot) / ORDER).astype(jnp.bfloat16)

    rot = jnp.where(is_left, left_rot, right_rot)
    product = jnp.dot(stat_new, rot, preferred_element_type=jnp.float32)
    squares = jnp.sum(product * product, axis=0)
    current = (product / jnp.sqrt(squares / ORDER + NORM_EPS)).astype(jnp.bfloat16)
    for _ in range(NS_ITERS - 1):
        gram = (contract_cols(current, current) / ORDER).astype(jnp.bfloat16)
        current = (
            1.5 * current.astype(jnp.float32)
            - 0.5 * jnp.dot(gram, current, preferred_element_type=jnp.float32)
        ).astype(jnp.bfloat16)
    rows = lax.dynamic_slice_in_dim(current, row_start, ROWS, 0)
    gram = (contract_cols(rows, current) / ORDER).astype(jnp.bfloat16)
    result = 1.5 * rows.astype(jnp.float32) - 0.5 * jnp.dot(
        gram, current, preferred_element_type=jnp.float32
    )
    size = lax.axis_size("dp")
    other = lax.ppermute(result, "dp", [(i, i ^ 1) for i in range(size)])
    left_result = jnp.where(is_left, result, other)
    right_result = jnp.where(is_left, other, result)
    return (update, second_new, left_result, right_result)


def solution(mesh):
    return jax.shard_map(
        body,
        mesh=mesh,
        in_specs=(
            P("dp", "shard", None),
            P("shard", None),
            P(None, "shard"),
            P("shard", None),
            P("shard", None),
            P("shard", None),
            P("shard", None),
        ),
        out_specs=(P("shard", None), P(None, "shard"), P("shard", None), P("shard", None)),
        check_vma=False,
    )
```

```python
import jax
import jax.numpy as jnp
from jax import lax
from jax.experimental import pallas as pl
from jax.experimental.pallas import tpu as pltpu
from jax.sharding import PartitionSpec as P

NS_ITERS = 2


BETA_ONE = 0.9
BETA_TWO = 0.9
BETA_STAT = 0.95
EPSILON = 1e-08
NORM_EPS = 1e-06

ORDER = 1024
SHARDS = 8
ROWS = ORDER // SHARDS
SIDE = 4
COLS = ORDER // SIDE
COPIES = 120
LOCALS = 13


def contract_rows(left_mat, right_mat):
    return lax.dot_general(
        left_mat, right_mat, (((0,), (0,)), ((), ())), preferred_element_type=jnp.float32
    )


def contract_cols(left_mat, right_mat):
    return lax.dot_general(
        left_mat, right_mat, (((1,), (1,)), ((), ())), preferred_element_type=jnp.float32
    )


class Place:
    def __init__(self):
        data = lax.axis_index("dp")
        self.z = lax.axis_index("shard")
        self.core = lax.rem(data, 2)
        self.zhi = lax.rem(lax.div(data, 2), 2)
        y = lax.rem(lax.div(data, 4), 4)
        x = lax.div(data, 16)
        self.p = x + self.core * (y - x)
        self.q = y + self.core * (x - y)

    def at(self, p, q, zhi, core):
        x = p + self.core * (q - p)
        y = q + self.core * (p - q)
        return ((x * 4 + y) * 2 + zhi) * 2 + core

    def along_p(self, step):
        p = lax.rem(self.p + step, SIDE)
        return (self.at(p, self.q, self.zhi, self.core), self.z)

    def along_q(self, step):
        q = lax.rem(self.q + step, SIDE)
        return (self.at(self.p, q, self.zhi, self.core), self.z)

    def along_z(self, step):
        z = lax.rem(self.z + step, SHARDS)
        return (self.at(self.p, self.q, self.zhi, self.core), z)

    def far(self):
        return (self.at(self.p, self.q, 1 - self.zhi, self.core), self.z)

    def sibling(self):
        return (self.at(self.p, self.q, self.zhi, 1 - self.core), self.z)


class Copies:
    def __init__(self, send, recv):
        self.send, self.recv, self.count, self.started = send, recv, 0, []

    def start(self, src, dst, device):
        copy = pltpu.make_async_remote_copy(
            src_ref=src,
            dst_ref=dst,
            send_sem=self.send.at[self.count],
            recv_sem=self.recv.at[self.count],
            device_id=device,
            device_id_type=pl.DeviceIdType.MESH,
        )
        self.count += 1
        copy.start()
        self.started.append(copy)
        return copy

    def finish(self):
        for copy in self.started:
            copy.wait_send()


class Ring:
    def __init__(self, copies, spot, along):
        self.copies, self.spot, self.along = copies, spot, along

    def first(self):
        own = self.spot(0, pl.ds(0, SHARDS))
        self.stage = [
            self.copies.start(own, own, self.along(1)),
            self.copies.start(own, own, self.along(3)),
        ]

    def second(self):
        self.arrived()
        low, high = pl.ds(0, SHARDS // 2), pl.ds(SHARDS // 2, SHARDS // 2)
        self.stage = [
            self.copies.start(self.spot(3, low), self.spot(3, low), self.along(1)),
            self.copies.start(self.spot(1, high), self.spot(1, high), self.along(3)),
        ]

    def arrived(self):
        for copy in self.stage:
            copy.wait_recv()


class Spread:
    def __init__(self, place, copies, piece, spot, local_sem):
        self.local = pltpu.make_async_copy(piece, spot, local_sem)
        self.local.start()
        self.stage = [
            copies.start(piece, spot, place.along_z(step)) for step in (7, 1, 6, 2, 5, 3, 4)
        ]

    def arrived(self):
        self.local.wait()
        for copy in self.stage:
            copy.wait_recv()


class Gather:
    def __init__(self, place, copies, local_sem, out):
        self.place, self.copies, self.local_sem, self.out = place, copies, local_sem, out
        self.q_ring = Ring(copies, self.q_spot, place.along_q)
        self.p_ring = Ring(copies, self.p_spot, place.along_p)
        self.to_core = []

    def rows(self, p):
        height = ROWS // SIDE // 2
        start = self.place.core * (ROWS // 2) + p * height
        return pl.ds(pl.multiple_of(start, height), height)

    def piece(self, ref):
        return ref.at[self.rows(self.place.p), cols(self.place.q)]

    def z_stage(self, piece):
        place = self.place
        spot = self.out.at[place.z, self.rows(place.p), cols(place.q)]
        self.spread = Spread(place, self.copies, piece, spot, self.local_sem)

    def q_spot(self, step, zs):
        q = lax.rem(self.place.q + step, SIDE)
        return self.out.at[zs, self.rows(self.place.p), cols(q)]

    def p_spot(self, step, zs):
        p = lax.rem(self.place.p + step, SIDE)
        return self.out.at[zs, self.rows(p), :]

    def q_first(self):
        self.spread.arrived()
        self.q_ring.first()

    def q_second(self):
        self.q_ring.second()

    def q_third(self):
        self.q_ring.arrived()

    def p_first(self):
        self.p_ring.first()
        self.share(0)

    def p_second(self):
        self.p_ring.second()
        self.share(1)
        self.share(3)

    def p_third(self):
        self.p_ring.arrived()
        self.share(2)

    def finish(self):
        for copy in self.to_core:
            copy.wait_recv()

    def share(self, step):
        block = self.p_spot(step, pl.ds(0, SHARDS))
        self.to_core.append(self.copies.start(block, block, self.place.sibling()))


def cols(q):
    return pl.ds(pl.multiple_of(q * COLS, COLS), COLS)


def columns_of(ref, index):
    return ref[:, :, cols(index)].reshape(ORDER, COLS)


def rows_of(ref, index):
    return ref[pl.ds(2 * index, 2)].reshape(COLS, ORDER)


def full(ref):
    return ref[...].reshape(ORDER, ORDER)


def multiply(left_mat, right_mat):
    return jnp.dot(left_mat, right_mat, preferred_element_type=jnp.float32)


def rotate(left_rot, turned, second, out_second, scaled):
    @pl.loop(0, SIDE)
    def _(index):
        rotated = contract_rows(columns_of(left_rot, index), turned[...].reshape(ORDER, COLS))
        rotated = rotated / ORDER
        grad_rot, moment_rot = rotated[:, :ROWS], rotated[:, ROWS:]
        new = BETA_TWO * second[cols(index), :] + (1.0 - BETA_TWO) * grad_rot * grad_rot
        out_second[cols(index), :] = new
        scaled[cols(index), :] = (moment_rot / (jnp.sqrt(new) + EPSILON)).astype(jnp.bfloat16)


def turn_back(left_rot, scaled, back):
    @pl.loop(0, SIDE)
    def _(index):
        back[pl.ds(2 * index, 2)] = (
            multiply(rows_of(left_rot, index), scaled[...])
            .astype(jnp.bfloat16)
            .reshape(2, ROWS, ROWS)
        )


def power_step(stat, rot, current):
    @pl.loop(0, SIDE)
    def _(index):
        product = multiply(full(stat), columns_of(rot, index))
        squares = jnp.sum(product * product, axis=0, keepdims=True)
        start = product / jnp.sqrt(squares / ORDER + NORM_EPS)
        current[:, :, cols(index)] = start.astype(jnp.bfloat16).reshape(SHARDS, ROWS, COLS)


def newton_schulz(current, gram, later):
    @pl.loop(0, SIDE)
    def _(index):
        block = contract_cols(full(current), rows_of(current, index)) / ORDER
        gram[:, :, cols(index)] = block.astype(jnp.bfloat16).reshape(SHARDS, ROWS, COLS)

    @pl.loop(0, SIDE)
    def _(index):
        mine = columns_of(current, index)
        block = 1.5 * mine.astype(jnp.float32) - 0.5 * multiply(full(gram), mine)
        later[:, :, cols(index)] = block.astype(jnp.bfloat16).reshape(SHARDS, ROWS, COLS)


def renew_stat(place, grad, stat, out):
    mine = cols(place.q)

    def keep(pair, outer):
        new = BETA_STAT * stat[pair] + (1.0 - BETA_STAT) * outer.reshape(2, ROWS, COLS)
        out[pair, :, mine] = new.astype(jnp.bfloat16)

    @pl.when(place.core == 0)
    def _():
        other = grad[pl.ds(2 * place.q, 2)].reshape(COLS, ORDER)

        @pl.loop(0, SHARDS // 2)
        def _(index):
            pair = pl.ds(2 * index, 2)
            keep(pair, contract_cols(grad[pair].reshape(COLS, ORDER), other))

    @pl.when(place.core == 1)
    def _():
        other = grad[:, :, mine].reshape(ORDER, COLS)

        @pl.loop(0, SHARDS // 2)
        def _(index):
            block = grad[:, :, cols(index)].reshape(ORDER, COLS)
            keep(pl.ds(2 * index, 2), contract_rows(block, other))


def step_kernel(
    grads, moment, second, stat_left, stat_right, base_left, base_right,
    out_update, out_second, out_bases,
    bases, all_grad, all_moment, all_turned, all_stat, new_stat,
    current, gram, later, gram_rows, scaled, back, back_rows,
    recv0, acc0, recv1, acc1, recv2, acc2, recv3, grad_piece, moment_piece,
    own_grads, own_second, old_moment, stat_pieces, base_pieces, sent_bases, stat_piece,
    send, recv, local,
):
    place = Place()
    half = ROWS // 2
    mine = pl.ds(pl.multiple_of(place.core * half, half), half)
    theirs = pl.ds(pl.multiple_of((1 - place.core) * half, half), half)

    def quarter(p):
        return pl.ds(pl.multiple_of(p * (ROWS // SIDE), ROWS // SIDE), ROWS // SIDE)

    copies = Copies(send, recv)
    g, m, l, r, t = [
        Gather(place, copies, local.at[index], out)
        for index, out in enumerate(
            (all_grad, all_moment, bases.at[0], bases.at[1], all_turned)
        )
    ]
    stat_spot = (quarter(place.p), cols(place.q))
    loads = [
        pltpu.make_async_copy(src, dst, local.at[6 + index])
        for index, (src, dst) in enumerate(
            (
                (l.piece(base_left), base_pieces.at[0]),
                (r.piece(base_right), base_pieces.at[1]),
                (stat_left.at[stat_spot], stat_pieces.at[0]),
                (stat_right.at[stat_spot], stat_pieces.at[1]),
                (grads.at[mine, :], own_grads),
                (g.piece(moment), old_moment),
                (second, own_second),
            )
        )
    ]
    for load in loads:
        load.start()

    for load in loads[:4]:
        load.wait()
    sent_bases[...] = base_pieces[...].astype(jnp.bfloat16)
    stat_piece[...] = stat_pieces[place.core]

    barrier = pltpu.get_barrier_semaphore()
    partners = [place.sibling(), place.far()]
    partners += [place.along_p(step) for step in (1, 2, 3)]
    partners += [place.along_q(step) for step in (1, 2, 3)]
    partners += [place.along_z(step) for step in range(1, SHARDS)]
    for partner in partners:
        pl.semaphore_signal(
            barrier, inc=1, device_id=partner, device_id_type=pl.DeviceIdType.MESH
        )
    pl.semaphore_wait(barrier, len(partners))

    def stat_p_spot(step, zs):
        return all_stat.at[zs, quarter(lax.rem(place.p + step, SIDE)), :]

    def stat_q_spot(step, zs):
        return new_stat.at[zs, :, cols(lax.rem(place.q + step, SIDE))]

    s_in = Ring(copies, stat_p_spot, place.along_p)
    s_out = Ring(copies, stat_q_spot, place.along_q)

    core_copy = copies.start(grads.at[theirs, :], recv0, place.sibling())
    l.z_stage(sent_bases.at[0])
    r.z_stage(sent_bases.at[1])
    s_spread = Spread(
        place,
        copies,
        stat_piece,
        all_stat.at[place.z, quarter(place.p), :],
        local.at[5],
    )

    loads[4].wait()
    core_copy.wait_recv()
    acc0[...] = (
        own_grads[...].astype(jnp.float32) + recv0[...].astype(jnp.float32)
    ).reshape(acc0.shape)
    p_copies = [
        copies.start(
            acc0.at[lax.rem(place.p + step, SIDE)], recv1.at[step - 1], place.along_p(step)
        )
        for step in (1, 3, 2)
    ]
    for copy in p_copies:
        copy.wait_recv()
    acc1[...] = (acc0[place.p] + recv1[0]) + (recv1[1] + recv1[2])
    q_copies = [
        copies.start(
            acc1.at[:, cols(lax.rem(place.q + step, SIDE))],
            recv2.at[step - 1],
            place.along_q(step),
        )
        for step in (1, 3, 2)
    ]
    for copy in q_copies:
        copy.wait_recv()
    acc2[...] = (acc1[:, cols(place.q)] + recv2[0]) + (recv2[1] + recv2[2])
    far_copy = copies.start(acc2, recv3, place.far())
    l.q_first()
    r.q_first()
    far_copy.wait_recv()
    piece = (acc2[...] + recv3[...]).astype(jnp.bfloat16)
    grad_piece[...] = piece
    loads[5].wait()
    old = old_moment[...]
    moment_piece[...] = (
        BETA_ONE * old + (1.0 - BETA_ONE) * piece.astype(jnp.float32)
    ).astype(jnp.bfloat16)
    g.z_stage(grad_piece)
    m.z_stage(moment_piece)

    l.q_second()
    r.q_second()
    l.q_third()
    l.p_first()
    r.q_third()
    r.p_first()
    s_spread.arrived()
    s_in.first()
    g.q_first()
    m.q_first()
    r.p_second()
    l.p_second()
    s_in.second()
    g.q_second()
    m.q_second()
    r.p_third()
    l.p_third()
    g.q_third()
    g.p_first()
    m.q_third()
    r.finish()
    own = g.rows(place.p)
    height = ROWS // SIDE // 2
    pair = jnp.concatenate(
        [all_grad[:, own, :].reshape(ROWS, ORDER), all_moment[:, own, :].reshape(ROWS, ORDER)]
    )
    right_cols = bases[1, :, :, pl.ds(pl.multiple_of(place.z * ROWS, ROWS), ROWS)]
    turned = jnp.dot(
        pair, right_cols.reshape(ORDER, ROWS), preferred_element_type=jnp.float32
    ).astype(jnp.bfloat16)
    all_turned[:, own, :ROWS] = turned[:ROWS].reshape(SHARDS, height, ROWS)
    all_turned[:, own, ROWS:] = turned[ROWS:].reshape(SHARDS, height, ROWS)
    g.p_second()
    t.p_first()
    g.p_third()
    t.p_second()
    s_in.arrived()
    g.finish()
    renew_stat(place, all_grad, all_stat, new_stat)
    s_out.first()
    t.p_third()
    l.finish()
    t.finish()
    loads[6].wait()
    left_rot, right_rot = bases.at[0], bases.at[1]
    rotate(left_rot, all_turned, own_second, out_second, scaled)
    s_out.second()
    turn_back(left_rot, scaled, back)
    here = pl.ds(pl.multiple_of(place.z * ROWS, ROWS), ROWS)
    back_copies = [
        copies.start(
            back.at[lax.rem(place.z + step, SHARDS)],
            back_rows.at[:, here],
            place.along_z(step),
        )
        for step in (7, 1, 6, 2, 5, 3, 4)
    ]
    back_rows[:, here] = back[place.z]
    s_out.arrived()

    rot = bases.at[place.core]
    power_step(new_stat, rot, current)
    for _ in range(NS_ITERS - 1):
        newton_schulz(current, gram, later)
        current, later = later, current
    rows = current[place.z]

    @pl.loop(0, SIDE)
    def _(index):
        block = contract_cols(rows, rows_of(current, index)) / ORDER
        gram_rows[:, cols(index)] = block.astype(jnp.bfloat16)

    result_copies = []
    for index in range(SIDE):
        span = slice(index * COLS, (index + 1) * COLS)
        out_bases[place.core, :, span] = 1.5 * rows[:, span].astype(jnp.float32) - 0.5 * multiply(
            gram_rows[...], current[:, :, span].reshape(ORDER, COLS)
        )
        block = out_bases.at[place.core, :, span]
        result_copies.append(copies.start(block, block, place.sibling()))

    for copy in back_copies:
        copy.wait_recv()

    @pl.loop(0, SIDE)
    def _(index):
        block = contract_cols(back_rows[...], rows_of(right_rot, index)) / ORDER
        out_update[:, cols(index)] = block.astype(jnp.bfloat16)

    for copy in result_copies:
        copy.wait_recv()
    copies.finish()


def step(*operands):
    whole = (SHARDS, ROWS, ORDER)
    part = (SHARDS, ROWS, COLS)
    height = ROWS // SIDE // 2
    f32, bf16 = jnp.float32, jnp.bfloat16
    return pl.pallas_call(
        step_kernel,
        out_shape=[
            jax.ShapeDtypeStruct((ROWS, ORDER), bf16),
            jax.ShapeDtypeStruct((ORDER, ROWS), f32),
            jax.ShapeDtypeStruct((2, ROWS, ORDER), f32),
        ],
        in_specs=[pl.BlockSpec(memory_space=pl.ANY)] * 7,
        out_specs=[pl.BlockSpec(memory_space=pltpu.VMEM)] * 3,
        scratch_shapes=[
            pltpu.VMEM((2, *whole), bf16),
            pltpu.VMEM(whole, bf16),
            pltpu.VMEM(whole, bf16),
            pltpu.VMEM(part, bf16),
            pltpu.VMEM(part, f32),
            pltpu.VMEM(whole, bf16),
            pltpu.VMEM(whole, bf16),
            pltpu.VMEM(whole, bf16),
            pltpu.VMEM(whole, bf16),
            pltpu.VMEM((ROWS, ORDER), bf16),
            pltpu.VMEM((ORDER, ROWS), bf16),
            pltpu.VMEM((SHARDS, ROWS, ROWS), bf16),
            pltpu.VMEM((ROWS, ORDER), bf16),
            pltpu.VMEM((ROWS // 2, ORDER), bf16),
            pltpu.VMEM((SIDE, height, ORDER), f32),
            pltpu.VMEM((SIDE - 1, height, ORDER), f32),
            pltpu.VMEM((height, ORDER), f32),
            pltpu.VMEM((SIDE - 1, height, COLS), f32),
            pltpu.VMEM((height, COLS), f32),
            pltpu.VMEM((height, COLS), f32),
            pltpu.VMEM((height, COLS), bf16),
            pltpu.VMEM((height, COLS), bf16),
            pltpu.VMEM((ROWS // 2, ORDER), bf16),
            pltpu.VMEM((ORDER, ROWS), f32),
            pltpu.VMEM((height, COLS), f32),
            pltpu.VMEM((2, 2 * height, COLS), f32),
            pltpu.VMEM((2, height, COLS), f32),
            pltpu.VMEM((2, height, COLS), bf16),
            pltpu.VMEM((2 * height, COLS), f32),
            pltpu.SemaphoreType.DMA((COPIES,)),
            pltpu.SemaphoreType.DMA((COPIES,)),
            pltpu.SemaphoreType.DMA((LOCALS,)),
        ],
        compiler_params=pltpu.CompilerParams(collective_id=0, has_side_effects=True),
        name="step",
    )(*operands)


def body(group_grads, moment, second, stat_left, stat_right, basis_left, basis_right):
    update, second_new, bases = step(
        group_grads[0], moment, second, stat_left, stat_right, basis_left, basis_right
    )
    return (update, second_new, bases[0], bases[1])


def solution(mesh):
    return jax.shard_map(
        body,
        mesh=mesh,
        in_specs=(
            P("dp", "shard", None),
            P("shard", None),
            P(None, "shard"),
            P("shard", None),
            P("shard", None),
            P("shard", None),
            P("shard", None),
        ),
        out_specs=(P("shard", None), P(None, "shard"), P("shard", None), P("shard", None)),
        check_vma=False,
    )
```

```python
import jax
import jax.numpy as jnp
from jax import lax
from jax.experimental import pallas as pl
from jax.experimental.pallas import tpu as pltpu
from jax.sharding import PartitionSpec as P

NS_ITERS = 2


BETA_ONE = 0.9
BETA_TWO = 0.9
BETA_STAT = 0.95
EPSILON = 1e-08
NORM_EPS = 1e-06

ORDER = 1024
SHARDS = 8
ROWS = ORDER // SHARDS
SIDE = 4
COLS = ORDER // SIDE
COPIES = 120
LOCALS = 13


def contract_rows(left_mat, right_mat):
    return lax.dot_general(
        left_mat, right_mat, (((0,), (0,)), ((), ())), preferred_element_type=jnp.float32
    )


def contract_cols(left_mat, right_mat):
    return lax.dot_general(
        left_mat, right_mat, (((1,), (1,)), ((), ())), preferred_element_type=jnp.float32
    )


class Place:
    def __init__(self):
        data = lax.axis_index("dp")
        self.z = lax.axis_index("shard")
        self.core = lax.rem(data, 2)
        self.zhi = lax.rem(lax.div(data, 2), 2)
        y = lax.rem(lax.div(data, 4), 4)
        x = lax.div(data, 16)
        self.p = x + self.core * (y - x)
        self.q = y + self.core * (x - y)

    def at(self, p, q, zhi, core):
        x = p + self.core * (q - p)
        y = q + self.core * (p - q)
        return ((x * 4 + y) * 2 + zhi) * 2 + core

    def along_p(self, step):
        p = lax.rem(self.p + step, SIDE)
        return (self.at(p, self.q, self.zhi, self.core), self.z)

    def along_q(self, step):
        q = lax.rem(self.q + step, SIDE)
        return (self.at(self.p, q, self.zhi, self.core), self.z)

    def along_z(self, step):
        z = lax.rem(self.z + step, SHARDS)
        return (self.at(self.p, self.q, self.zhi, self.core), z)

    def across_p(self, step):
        p = lax.rem(self.p + step, SIDE)
        return (self.at(p, self.q, self.zhi, 1 - self.core), self.z)

    def across_q(self, step):
        q = lax.rem(self.q + step, SIDE)
        return (self.at(self.p, q, self.zhi, 1 - self.core), self.z)

    def far(self):
        return (self.at(self.p, self.q, 1 - self.zhi, self.core), self.z)

    def sibling(self):
        return (self.at(self.p, self.q, self.zhi, 1 - self.core), self.z)


class Copies:
    def __init__(self, send, recv):
        self.send, self.recv, self.count, self.started = send, recv, 0, []

    def start(self, src, dst, device):
        copy = pltpu.make_async_remote_copy(
            src_ref=src,
            dst_ref=dst,
            send_sem=self.send.at[self.count],
            recv_sem=self.recv.at[self.count],
            device_id=device,
            device_id_type=pl.DeviceIdType.MESH,
        )
        self.count += 1
        copy.start()
        self.started.append(copy)
        return copy

    def finish(self):
        for copy in self.started:
            copy.wait_send()


class Ring:
    def __init__(self, copies, spot, along):
        self.copies, self.spot, self.along = copies, spot, along

    def first(self):
        own = self.spot(0, pl.ds(0, SHARDS))
        self.stage = [
            self.copies.start(own, own, self.along(1)),
            self.copies.start(own, own, self.along(3)),
        ]

    def second(self):
        self.arrived()
        low, high = pl.ds(0, SHARDS // 2), pl.ds(SHARDS // 2, SHARDS // 2)
        self.stage = [
            self.copies.start(self.spot(3, low), self.spot(3, low), self.along(1)),
            self.copies.start(self.spot(1, high), self.spot(1, high), self.along(3)),
        ]

    def arrived(self):
        for copy in self.stage:
            copy.wait_recv()


class Spread:
    def __init__(self, place, copies, piece, spot, local_sem):
        self.local = pltpu.make_async_copy(piece, spot, local_sem)
        self.local.start()
        self.stage = [
            copies.start(piece, spot, place.along_z(step)) for step in (7, 1, 6, 2, 5, 3, 4)
        ]

    def arrived(self):
        self.local.wait()
        for copy in self.stage:
            copy.wait_recv()


class Gather:
    def __init__(self, place, copies, local_sem, out):
        self.place, self.copies, self.local_sem, self.out = place, copies, local_sem, out
        self.q_ring = Ring(copies, self.q_spot, place.along_q)
        self.p_ring = Ring(copies, self.p_spot, place.along_p)
        self.to_core = []

    def rows(self, p):
        height = ROWS // SIDE // 2
        start = self.place.core * (ROWS // 2) + p * height
        return pl.ds(pl.multiple_of(start, height), height)

    def piece(self, ref):
        return ref.at[self.rows(self.place.p), cols(self.place.q)]

    def z_stage(self, piece):
        place = self.place
        spot = self.out.at[place.z, self.rows(place.p), cols(place.q)]
        self.spread = Spread(place, self.copies, piece, spot, self.local_sem)

    def q_spot(self, step, zs):
        q = lax.rem(self.place.q + step, SIDE)
        return self.out.at[zs, self.rows(self.place.p), cols(q)]

    def p_spot(self, step, zs):
        p = lax.rem(self.place.p + step, SIDE)
        return self.out.at[zs, self.rows(p), :]

    def q_first(self):
        self.spread.arrived()
        self.q_ring.first()

    def q_second(self):
        self.q_ring.second()

    def q_third(self):
        self.q_ring.arrived()

    def p_first(self):
        self.p_ring.first()
        self.share(0)

    def p_second(self):
        self.p_ring.second()
        self.share(1)
        self.share(3)

    def p_third(self):
        self.p_ring.arrived()
        self.share(2)

    def finish(self):
        for copy in self.to_core:
            copy.wait_recv()

    def share(self, step):
        block = self.p_spot(step, pl.ds(0, SHARDS))
        self.to_core.append(self.copies.start(block, block, self.place.sibling()))


def cols(q):
    if isinstance(q, int):
        return pl.ds(q * COLS, COLS)
    return pl.ds(pl.multiple_of(q * COLS, COLS), COLS)


def columns_of(ref, index):
    return ref[:, :, cols(index)].reshape(ORDER, COLS)


def rows_of(ref, index):
    return ref[pl.ds(2 * index, 2)].reshape(COLS, ORDER)


def full(ref):
    return ref[...].reshape(ORDER, ORDER)


def multiply(left_mat, right_mat):
    return jnp.dot(left_mat, right_mat, preferred_element_type=jnp.float32)


def rotate(left_rot, turned, second, out_second, scaled):
    for index in range(SIDE):
        rotated = contract_rows(columns_of(left_rot, index), turned[...].reshape(ORDER, COLS))
        rotated = rotated / ORDER
        grad_rot, moment_rot = rotated[:, :ROWS], rotated[:, ROWS:]
        new = BETA_TWO * second[cols(index), :] + (1.0 - BETA_TWO) * grad_rot * grad_rot
        out_second[cols(index), :] = new
        scaled[cols(index), :] = (moment_rot / (jnp.sqrt(new) + EPSILON)).astype(jnp.bfloat16)


def turn_back(left_rot, scaled, back):
    for index in range(SIDE):
        back[pl.ds(2 * index, 2)] = (
            multiply(rows_of(left_rot, index), scaled[...])
            .astype(jnp.bfloat16)
            .reshape(2, ROWS, ROWS)
        )


def quarter_product(place, stat, rot, steps, index):
    total = None
    for step in steps:
        part = lax.rem(place.q + step, SIDE)
        term = multiply(
            columns_of(stat, part), rot[pl.ds(2 * part, 2), :, cols(index)].reshape(COLS, COLS)
        )
        total = term if total is None else total + term
    return total


def normalize(product):
    squares = jnp.sum(product * product, axis=0, keepdims=True)
    start = product / jnp.sqrt(squares / ORDER + NORM_EPS)
    return start.astype(jnp.bfloat16).reshape(SHARDS, ROWS, COLS)


def newton_schulz(current, gram, later):
    for index in range(SIDE):
        block = contract_cols(full(current), rows_of(current, index)) / ORDER
        gram[:, :, cols(index)] = block.astype(jnp.bfloat16).reshape(SHARDS, ROWS, COLS)

    for index in range(SIDE):
        mine = columns_of(current, index)
        block = 1.5 * mine.astype(jnp.float32) - 0.5 * multiply(full(gram), mine)
        later[:, :, cols(index)] = block.astype(jnp.bfloat16).reshape(SHARDS, ROWS, COLS)


def renew_stat(place, grad, stat, out):
    mine = cols(place.q)

    def keep(pair, outer):
        new = BETA_STAT * stat[pair] + (1.0 - BETA_STAT) * outer.reshape(2, ROWS, COLS)
        out[pair, :, mine] = new.astype(jnp.bfloat16)

    @pl.when(place.core == 0)
    def _():
        other = grad[pl.ds(2 * place.q, 2)].reshape(COLS, ORDER)

        for index in range(SIDE):
            pair = pl.ds(2 * index, 2)
            keep(pair, contract_cols(grad[pair].reshape(COLS, ORDER), other))

    @pl.when(place.core == 1)
    def _():
        other = grad[:, :, mine].reshape(ORDER, COLS)

        for index in range(SIDE):
            block = grad[:, :, cols(index)].reshape(ORDER, COLS)
            keep(pl.ds(2 * index, 2), contract_rows(block, other))


def step_kernel(
    grads, moment, second, stat_left, stat_right, base_left, base_right,
    out_update, out_second, out_bases,
    bases, all_grad, all_moment, all_turned, all_stat, new_stat,
    current, gram, later, gram_rows, scaled, back, back_rows,
    product, recv1, acc1, recv2, acc2, recv3, grad_piece, moment_piece,
    own_grads, own_second, old_moment, stat_pieces, base_pieces, sent_bases, stat_piece,
    send, recv, local,
):
    place = Place()
    height = ROWS // SIDE // 2

    def quarter(p):
        return pl.ds(pl.multiple_of(p * (ROWS // SIDE), ROWS // SIDE), ROWS // SIDE)

    copies = Copies(send, recv)
    g, m, l, r, t = [
        Gather(place, copies, local.at[index], out)
        for index, out in enumerate(
            (all_grad, all_moment, bases.at[0], bases.at[1], all_turned)
        )
    ]
    stat_spot = (quarter(place.p), cols(place.q))
    loads = [
        pltpu.make_async_copy(src, dst, local.at[6 + index])
        for index, (src, dst) in enumerate(
            (
                (l.piece(base_left), base_pieces.at[0]),
                (r.piece(base_right), base_pieces.at[1]),
                (stat_left.at[stat_spot], stat_pieces.at[0]),
                (stat_right.at[stat_spot], stat_pieces.at[1]),
                (grads.at[g.rows(place.p), :], own_grads),
                (g.piece(moment), old_moment),
                (second, own_second),
            )
        )
    ]
    for load in loads:
        load.start()

    for load in loads[:4]:
        load.wait()
    sent_bases[...] = base_pieces[...].astype(jnp.bfloat16)
    stat_piece[...] = stat_pieces[place.core]

    barrier = pltpu.get_barrier_semaphore()
    partners = [place.sibling(), place.far()]
    partners += [place.along_p(step) for step in (1, 2, 3)]
    partners += [place.along_q(step) for step in (1, 2, 3)]
    partners += [place.across_p(step) for step in (1, 2, 3)]
    partners += [place.across_q(step) for step in (1, 2, 3)]
    partners += [place.along_z(step) for step in range(1, SHARDS)]
    for partner in partners:
        pl.semaphore_signal(
            barrier, inc=1, device_id=partner, device_id_type=pl.DeviceIdType.MESH
        )
    pl.semaphore_wait(barrier, len(partners))

    def stat_p_spot(step, zs):
        return all_stat.at[zs, quarter(lax.rem(place.p + step, SIDE)), :]

    def stat_q_spot(step, zs):
        return new_stat.at[zs, :, cols(lax.rem(place.q + step, SIDE))]

    s_in = Ring(copies, stat_p_spot, place.along_p)
    s_out = Ring(copies, stat_q_spot, place.along_q)

    def other_rows(p):
        start = (1 - place.core) * (ROWS // 2) + p * height
        return pl.ds(pl.multiple_of(start, height), height)

    sum_copies = [
        copies.start(
            grads.at[g.rows(lax.rem(place.p + step, SIDE)), :],
            recv1.at[step - 1],
            place.along_p(step),
        )
        for step in (1, 3, 2)
    ]
    sum_copies += [
        copies.start(
            grads.at[other_rows(lax.rem(place.q + step, SIDE)), :],
            recv1.at[3 + step],
            place.across_q(step),
        )
        for step in (0, 1, 3, 2)
    ]
    l.z_stage(sent_bases.at[0])
    r.z_stage(sent_bases.at[1])
    s_spread = Spread(
        place,
        copies,
        stat_piece,
        all_stat.at[place.z, quarter(place.p), :],
        local.at[5],
    )

    loads[4].wait()
    for copy in sum_copies:
        copy.wait_recv()
    total = own_grads[...].astype(jnp.float32)
    for index in range(7):
        total = total + recv1[index].astype(jnp.float32)
    acc1[...] = total
    q_copies = [
        copies.start(
            acc1.at[:, cols(lax.rem(place.q + step, SIDE))],
            recv2.at[step - 1],
            place.along_q(step),
        )
        for step in (1, 3, 2)
    ]
    for copy in q_copies:
        copy.wait_recv()
    acc2[...] = (acc1[:, cols(place.q)] + recv2[0]) + (recv2[1] + recv2[2])
    far_copy = copies.start(acc2, recv3, place.far())
    l.q_first()
    r.q_first()
    far_copy.wait_recv()
    piece = (acc2[...] + recv3[...]).astype(jnp.bfloat16)
    grad_piece[...] = piece
    loads[5].wait()
    old = old_moment[...]
    moment_piece[...] = (
        BETA_ONE * old + (1.0 - BETA_ONE) * piece.astype(jnp.float32)
    ).astype(jnp.bfloat16)
    g.z_stage(grad_piece)
    m.z_stage(moment_piece)

    l.q_second()
    r.q_second()
    l.q_third()
    l.p_first()
    r.q_third()
    r.p_first()
    s_spread.arrived()
    s_in.first()
    g.q_first()
    m.q_first()
    r.p_second()
    l.p_second()
    s_in.second()
    g.q_second()
    m.q_second()
    r.p_third()
    l.p_third()
    g.q_third()
    g.p_first()
    m.q_third()
    r.finish()
    own = g.rows(place.p)
    pair = jnp.concatenate(
        [all_grad[:, own, :].reshape(ROWS, ORDER), all_moment[:, own, :].reshape(ROWS, ORDER)]
    )
    right_cols = bases[1, :, :, pl.ds(pl.multiple_of(place.z * ROWS, ROWS), ROWS)]
    turned = jnp.dot(
        pair, right_cols.reshape(ORDER, ROWS), preferred_element_type=jnp.float32
    ).astype(jnp.bfloat16)
    all_turned[:, own, :ROWS] = turned[:ROWS].reshape(SHARDS, height, ROWS)
    all_turned[:, own, ROWS:] = turned[ROWS:].reshape(SHARDS, height, ROWS)
    g.p_second()
    t.p_first()
    g.p_third()
    t.p_second()
    s_in.arrived()
    g.finish()
    renew_stat(place, all_grad, all_stat, new_stat)
    s_out.first()
    l.finish()
    left_rot, right_rot, rot = bases.at[0], bases.at[1], bases.at[place.core]
    for index in range(SIDE):
        product[:, cols(index)] = quarter_product(place, new_stat, rot, (0,), index)
    t.p_third()
    t.finish()
    loads[6].wait()
    rotate(left_rot, all_turned, own_second, out_second, scaled)
    s_out.second()
    turn_back(left_rot, scaled, back)
    here = pl.ds(pl.multiple_of(place.z * ROWS, ROWS), ROWS)
    back_copies = [
        copies.start(
            back.at[lax.rem(place.z + step, SHARDS)],
            back_rows.at[:, here],
            place.along_z(step),
        )
        for step in (7, 1, 6, 2, 5, 3, 4)
    ]
    back_rows[:, here] = back[place.z]
    for index in range(SIDE):
        product[:, cols(index)] += quarter_product(place, new_stat, rot, (1, 3), index)
    s_out.arrived()
    for index in range(SIDE):
        whole = product[:, cols(index)] + quarter_product(place, new_stat, rot, (2,), index)
        current[:, :, cols(index)] = normalize(whole)
    for _ in range(NS_ITERS - 1):
        newton_schulz(current, gram, later)
        current, later = later, current
    rows = current[place.z]

    for index in range(SIDE):
        block = contract_cols(rows, rows_of(current, index)) / ORDER
        gram_rows[:, cols(index)] = block.astype(jnp.bfloat16)

    result_copies = []
    for index in range(SIDE):
        span = slice(index * COLS, (index + 1) * COLS)
        out_bases[place.core, :, span] = 1.5 * rows[:, span].astype(jnp.float32) - 0.5 * multiply(
            gram_rows[...], current[:, :, span].reshape(ORDER, COLS)
        )
        block = out_bases.at[place.core, :, span]
        result_copies.append(copies.start(block, block, place.sibling()))

    for copy in back_copies:
        copy.wait_recv()

    for index in range(SIDE):
        block = contract_cols(back_rows[...], rows_of(right_rot, index)) / ORDER
        out_update[:, cols(index)] = block.astype(jnp.bfloat16)

    for copy in result_copies:
        copy.wait_recv()
    copies.finish()


def step(*operands):
    whole = (SHARDS, ROWS, ORDER)
    part = (SHARDS, ROWS, COLS)
    height = ROWS // SIDE // 2
    f32, bf16 = jnp.float32, jnp.bfloat16
    return pl.pallas_call(
        step_kernel,
        out_shape=[
            jax.ShapeDtypeStruct((ROWS, ORDER), bf16),
            jax.ShapeDtypeStruct((ORDER, ROWS), f32),
            jax.ShapeDtypeStruct((2, ROWS, ORDER), f32),
        ],
        in_specs=[pl.BlockSpec(memory_space=pl.ANY)] * 7,
        out_specs=[pl.BlockSpec(memory_space=pltpu.VMEM)] * 3,
        scratch_shapes=[
            pltpu.VMEM((2, *whole), bf16),
            pltpu.VMEM(whole, bf16),
            pltpu.VMEM(whole, bf16),
            pltpu.VMEM(part, bf16),
            pltpu.VMEM(part, f32),
            pltpu.VMEM(whole, bf16),
            pltpu.VMEM(whole, bf16),
            pltpu.VMEM(whole, bf16),
            pltpu.VMEM(whole, bf16),
            pltpu.VMEM((ROWS, ORDER), bf16),
            pltpu.VMEM((ORDER, ROWS), bf16),
            pltpu.VMEM((SHARDS, ROWS, ROWS), bf16),
            pltpu.VMEM((ROWS, ORDER), bf16),
            pltpu.VMEM((ORDER, ORDER), f32),
            pltpu.VMEM((7, height, ORDER), bf16),
            pltpu.VMEM((height, ORDER), f32),
            pltpu.VMEM((SIDE - 1, height, COLS), f32),
            pltpu.VMEM((height, COLS), f32),
            pltpu.VMEM((height, COLS), f32),
            pltpu.VMEM((height, COLS), bf16),
            pltpu.VMEM((height, COLS), bf16),
            pltpu.VMEM((height, ORDER), bf16),
            pltpu.VMEM((ORDER, ROWS), f32),
            pltpu.VMEM((height, COLS), f32),
            pltpu.VMEM((2, 2 * height, COLS), f32),
            pltpu.VMEM((2, height, COLS), f32),
            pltpu.VMEM((2, height, COLS), bf16),
            pltpu.VMEM((2 * height, COLS), f32),
            pltpu.SemaphoreType.DMA((COPIES,)),
            pltpu.SemaphoreType.DMA((COPIES,)),
            pltpu.SemaphoreType.DMA((LOCALS,)),
        ],
        compiler_params=pltpu.CompilerParams(collective_id=0, has_side_effects=True),
        name="step",
    )(*operands)


def deliver_kernel(
    update, second, bases, out_update, out_second, out_left, out_right,
    held_update, held_second, held_bases, sems_in, sems_out,
):
    routes = (
        (bases.at[0], held_bases.at[0], out_left),
        (bases.at[1], held_bases.at[1], out_right),
        (second, held_second, out_second),
        (update, held_update, out_update),
    )
    loads = [
        pltpu.make_async_copy(src, held, sems_in.at[index])
        for index, (src, held, _) in enumerate(routes)
    ]
    stores = [
        pltpu.make_async_copy(held, dst, sems_out.at[index])
        for index, (_, held, dst) in enumerate(routes)
    ]
    for load in loads:
        load.start()
    for load, store in zip(loads, stores):
        load.wait()
        store.start()
    for store in stores:
        store.wait()


def deliver(update, second, bases):
    one = jax.ShapeDtypeStruct(bases.shape[1:], bases.dtype)
    outs = [jax.ShapeDtypeStruct(array.shape, array.dtype) for array in (update, second)]
    return pl.pallas_call(
        deliver_kernel,
        out_shape=[*outs, one, one],
        in_specs=[pl.BlockSpec(memory_space=pl.ANY)] * 3,
        out_specs=[pl.BlockSpec(memory_space=pl.ANY)] * 4,
        scratch_shapes=[
            pltpu.VMEM(update.shape, update.dtype),
            pltpu.VMEM(second.shape, second.dtype),
            pltpu.VMEM(bases.shape, bases.dtype),
            pltpu.SemaphoreType.DMA((4,)),
            pltpu.SemaphoreType.DMA((4,)),
        ],
        name="deliver",
    )(update, second, bases)


def body(group_grads, moment, second, stat_left, stat_right, basis_left, basis_right):
    update, second_new, bases = step(
        group_grads[0], moment, second, stat_left, stat_right, basis_left, basis_right
    )
    return tuple(deliver(update, second_new, bases))


def solution(mesh):
    return jax.shard_map(
        body,
        mesh=mesh,
        in_specs=(
            P("dp", "shard", None),
            P("shard", None),
            P(None, "shard"),
            P("shard", None),
            P("shard", None),
            P("shard", None),
            P("shard", None),
        ),
        out_specs=(P("shard", None), P(None, "shard"), P("shard", None), P("shard", None)),
        check_vma=False,
    )
```

```python
import jax
import jax.numpy as jnp
from jax import lax
from jax.experimental import pallas as pl
from jax.experimental.pallas import tpu as pltpu
from jax.sharding import PartitionSpec as P

NS_ITERS = 2


BETA_ONE = 0.9
BETA_TWO = 0.9
BETA_STAT = 0.95
EPSILON = 1e-08
NORM_EPS = 1e-06

ORDER = 1024
SHARDS = 8
ROWS = ORDER // SHARDS
SIDE = 4
COLS = ORDER // SIDE
COPIES = 120
LOCALS = 13


def contract_rows(left_mat, right_mat):
    return lax.dot_general(
        left_mat, right_mat, (((0,), (0,)), ((), ())), preferred_element_type=jnp.float32
    )


def contract_cols(left_mat, right_mat):
    return lax.dot_general(
        left_mat, right_mat, (((1,), (1,)), ((), ())), preferred_element_type=jnp.float32
    )


class Place:
    def __init__(self):
        data = lax.axis_index("dp")
        self.z = lax.axis_index("shard")
        self.core = lax.rem(data, 2)
        self.zhi = lax.rem(lax.div(data, 2), 2)
        y = lax.rem(lax.div(data, 4), 4)
        x = lax.div(data, 16)
        self.p = x + self.core * (y - x)
        self.q = y + self.core * (x - y)

    def at(self, p, q, zhi, core):
        x = p + self.core * (q - p)
        y = q + self.core * (p - q)
        return ((x * 4 + y) * 2 + zhi) * 2 + core

    def along_p(self, step):
        p = lax.rem(self.p + step, SIDE)
        return (self.at(p, self.q, self.zhi, self.core), self.z)

    def along_q(self, step):
        q = lax.rem(self.q + step, SIDE)
        return (self.at(self.p, q, self.zhi, self.core), self.z)

    def along_z(self, step):
        z = lax.rem(self.z + step, SHARDS)
        return (self.at(self.p, self.q, self.zhi, self.core), z)

    def across_p(self, step):
        p = lax.rem(self.p + step, SIDE)
        return (self.at(p, self.q, self.zhi, 1 - self.core), self.z)

    def across_q(self, step):
        q = lax.rem(self.q + step, SIDE)
        return (self.at(self.p, q, self.zhi, 1 - self.core), self.z)

    def far(self):
        return (self.at(self.p, self.q, 1 - self.zhi, self.core), self.z)

    def sibling(self):
        return (self.at(self.p, self.q, self.zhi, 1 - self.core), self.z)


class Copies:
    def __init__(self, send, recv):
        self.send, self.recv, self.count, self.started = send, recv, 0, []

    def start(self, src, dst, device):
        copy = pltpu.make_async_remote_copy(
            src_ref=src,
            dst_ref=dst,
            send_sem=self.send.at[self.count],
            recv_sem=self.recv.at[self.count],
            device_id=device,
            device_id_type=pl.DeviceIdType.MESH,
        )
        self.count += 1
        copy.start()
        self.started.append(copy)
        return copy

    def finish(self):
        for copy in self.started:
            copy.wait_send()


class Ring:
    def __init__(self, copies, spot, along):
        self.copies, self.spot, self.along = copies, spot, along

    def first(self):
        own = self.spot(0, pl.ds(0, SHARDS))
        self.stage = [
            self.copies.start(own, own, self.along(1)),
            self.copies.start(own, own, self.along(3)),
        ]

    def second(self):
        self.arrived()
        low, high = pl.ds(0, SHARDS // 2), pl.ds(SHARDS // 2, SHARDS // 2)
        self.stage = [
            self.copies.start(self.spot(3, low), self.spot(3, low), self.along(1)),
            self.copies.start(self.spot(1, high), self.spot(1, high), self.along(3)),
        ]

    def arrived(self):
        for copy in self.stage:
            copy.wait_recv()


class Spread:
    def __init__(self, place, copies, piece, spot, local_sem):
        self.local = pltpu.make_async_copy(piece, spot, local_sem)
        self.local.start()
        self.stage = [
            copies.start(piece, spot, place.along_z(step)) for step in (7, 1, 6, 2, 5, 3, 4)
        ]

    def arrived(self):
        self.local.wait()
        for copy in self.stage:
            copy.wait_recv()


class Gather:
    def __init__(self, place, copies, local_sem, out):
        self.place, self.copies, self.local_sem, self.out = place, copies, local_sem, out
        self.q_ring = Ring(copies, self.q_spot, place.along_q)
        self.p_ring = Ring(copies, self.p_spot, place.along_p)
        self.to_core = []

    def rows(self, p):
        height = ROWS // SIDE // 2
        start = self.place.core * (ROWS // 2) + p * height
        return pl.ds(pl.multiple_of(start, height), height)

    def piece(self, ref):
        return ref.at[self.rows(self.place.p), cols(self.place.q)]

    def z_stage(self, piece):
        place = self.place
        spot = self.out.at[place.z, self.rows(place.p), cols(place.q)]
        self.spread = Spread(place, self.copies, piece, spot, self.local_sem)

    def q_spot(self, step, zs):
        q = lax.rem(self.place.q + step, SIDE)
        return self.out.at[zs, self.rows(self.place.p), cols(q)]

    def p_spot(self, step, zs):
        p = lax.rem(self.place.p + step, SIDE)
        return self.out.at[zs, self.rows(p), :]

    def q_first(self):
        self.spread.arrived()
        self.q_ring.first()

    def q_second(self):
        self.q_ring.second()

    def q_third(self):
        self.q_ring.arrived()

    def p_first(self):
        self.p_ring.first()
        self.share(0)

    def p_second(self):
        self.p_ring.second()
        self.share(1)
        self.share(3)

    def p_third(self):
        self.p_ring.arrived()
        self.share(2)

    def finish(self):
        for copy in self.to_core:
            copy.wait_recv()

    def share(self, step):
        block = self.p_spot(step, pl.ds(0, SHARDS))
        self.to_core.append(self.copies.start(block, block, self.place.sibling()))


def cols(q):
    if isinstance(q, int):
        return pl.ds(q * COLS, COLS)
    return pl.ds(pl.multiple_of(q * COLS, COLS), COLS)


def columns_of(ref, index):
    return ref[:, :, cols(index)].reshape(ORDER, COLS)


def rows_of(ref, index):
    return ref[pl.ds(2 * index, 2)].reshape(COLS, ORDER)


def full(ref):
    return ref[...].reshape(ORDER, ORDER)


def multiply(left_mat, right_mat):
    return jnp.dot(left_mat, right_mat, preferred_element_type=jnp.float32)


def rotate(left_rot, turned, second, out_second, scaled):
    for index in range(SIDE):
        rotated = contract_rows(columns_of(left_rot, index), turned[...].reshape(ORDER, COLS))
        rotated = rotated / ORDER
        grad_rot, moment_rot = rotated[:, :ROWS], rotated[:, ROWS:]
        new = BETA_TWO * second[cols(index), :] + (1.0 - BETA_TWO) * grad_rot * grad_rot
        out_second[cols(index), :] = new
        scaled[cols(index), :] = (moment_rot / (jnp.sqrt(new) + EPSILON)).astype(jnp.bfloat16)


def quarter_product(place, stat, rot, steps, index):
    total = None
    for step in steps:
        part = lax.rem(place.q + step, SIDE)
        term = multiply(
            columns_of(stat, part), rot[pl.ds(2 * part, 2), :, cols(index)].reshape(COLS, COLS)
        )
        total = term if total is None else total + term
    return total


def normalize(product):
    squares = jnp.sum(product * product, axis=0, keepdims=True)
    start = product / jnp.sqrt(squares / ORDER + NORM_EPS)
    return start.astype(jnp.bfloat16).reshape(SHARDS, ROWS, COLS)


def newton_schulz(current, gram, later):
    for index in range(SIDE):
        block = contract_cols(full(current), rows_of(current, index)) / ORDER
        gram[:, :, cols(index)] = block.astype(jnp.bfloat16).reshape(SHARDS, ROWS, COLS)

    for index in range(SIDE):
        mine = columns_of(current, index)
        block = 1.5 * mine.astype(jnp.float32) - 0.5 * multiply(full(gram), mine)
        later[:, :, cols(index)] = block.astype(jnp.bfloat16).reshape(SHARDS, ROWS, COLS)


def renew_stat(place, grad, stat, out):
    mine = cols(place.q)

    def keep(pair, outer):
        new = BETA_STAT * stat[pair] + (1.0 - BETA_STAT) * outer.reshape(2, ROWS, COLS)
        out[pair, :, mine] = new.astype(jnp.bfloat16)

    @pl.when(place.core == 0)
    def _():
        other = grad[pl.ds(2 * place.q, 2)].reshape(COLS, ORDER)

        for index in range(SIDE):
            pair = pl.ds(2 * index, 2)
            keep(pair, contract_cols(grad[pair].reshape(COLS, ORDER), other))

    @pl.when(place.core == 1)
    def _():
        other = grad[:, :, mine].reshape(ORDER, COLS)

        for index in range(SIDE):
            block = grad[:, :, cols(index)].reshape(ORDER, COLS)
            keep(pl.ds(2 * index, 2), contract_rows(block, other))


def step_kernel(
    grads, moment, second, stat_left, stat_right, base_left, base_right,
    out_update, out_second, out_bases,
    bases, all_grad, all_moment, all_turned, all_stat, new_stat,
    current, gram, later, gram_rows, scaled, back, back_rows,
    product, recv1, acc1, recv2, acc2, recv3, grad_piece, moment_piece,
    own_grads, own_second, old_moment, stat_pieces, base_pieces, sent_bases, stat_piece,
    send, recv, local,
):
    place = Place()
    height = ROWS // SIDE // 2

    def quarter(p):
        return pl.ds(pl.multiple_of(p * (ROWS // SIDE), ROWS // SIDE), ROWS // SIDE)

    copies = Copies(send, recv)
    g, m, l, r, t = [
        Gather(place, copies, local.at[index], out)
        for index, out in enumerate(
            (all_grad, all_moment, bases.at[0], bases.at[1], all_turned)
        )
    ]
    stat_spot = (quarter(place.p), cols(place.q))
    loads = [
        pltpu.make_async_copy(src, dst, local.at[6 + index])
        for index, (src, dst) in enumerate(
            (
                (l.piece(base_left), base_pieces.at[0]),
                (r.piece(base_right), base_pieces.at[1]),
                (stat_left.at[stat_spot], stat_pieces.at[0]),
                (stat_right.at[stat_spot], stat_pieces.at[1]),
                (grads.at[g.rows(place.p), :], own_grads),
                (g.piece(moment), old_moment),
                (second, own_second),
            )
        )
    ]
    for load in loads:
        load.start()

    for load in loads[:4]:
        load.wait()
    sent_bases[...] = base_pieces[...].astype(jnp.bfloat16)
    stat_piece[...] = stat_pieces[place.core]

    barrier = pltpu.get_barrier_semaphore()
    partners = [place.sibling(), place.far()]
    partners += [place.along_p(step) for step in (1, 2, 3)]
    partners += [place.along_q(step) for step in (1, 2, 3)]
    partners += [place.across_p(step) for step in (1, 2, 3)]
    partners += [place.across_q(step) for step in (1, 2, 3)]
    partners += [place.along_z(step) for step in range(1, SHARDS)]
    for partner in partners:
        pl.semaphore_signal(
            barrier, inc=1, device_id=partner, device_id_type=pl.DeviceIdType.MESH
        )
    pl.semaphore_wait(barrier, len(partners))

    def stat_p_spot(step, zs):
        return all_stat.at[zs, quarter(lax.rem(place.p + step, SIDE)), :]

    def stat_q_spot(step, zs):
        return new_stat.at[zs, :, cols(lax.rem(place.q + step, SIDE))]

    s_in = Ring(copies, stat_p_spot, place.along_p)
    s_out = Ring(copies, stat_q_spot, place.along_q)

    def other_rows(p):
        start = (1 - place.core) * (ROWS // 2) + p * height
        return pl.ds(pl.multiple_of(start, height), height)

    sum_copies = [
        copies.start(
            grads.at[g.rows(lax.rem(place.p + step, SIDE)), :],
            recv1.at[step - 1],
            place.along_p(step),
        )
        for step in (1, 3, 2)
    ]
    sum_copies += [
        copies.start(
            grads.at[other_rows(lax.rem(place.q + step, SIDE)), :],
            recv1.at[3 + step],
            place.across_q(step),
        )
        for step in (0, 1, 3, 2)
    ]
    l.z_stage(sent_bases.at[0])
    r.z_stage(sent_bases.at[1])
    loads[4].wait()
    for copy in sum_copies:
        copy.wait_recv()
    total = own_grads[...].astype(jnp.float32)
    for index in range(7):
        total = total + recv1[index].astype(jnp.float32)
    acc1[...] = total
    q_copies = [
        copies.start(
            acc1.at[:, cols(lax.rem(place.q + step, SIDE))],
            recv2.at[step - 1],
            place.along_q(step),
        )
        for step in (1, 3, 2)
    ]
    for copy in q_copies:
        copy.wait_recv()
    acc2[...] = (acc1[:, cols(place.q)] + recv2[0]) + (recv2[1] + recv2[2])
    far_copy = copies.start(acc2, recv3, place.far())
    l.q_first()
    r.q_first()
    l.q_second()
    r.q_second()
    far_copy.wait_recv()
    piece = (acc2[...] + recv3[...]).astype(jnp.bfloat16)
    grad_piece[...] = piece
    loads[5].wait()
    old = old_moment[...]
    moment_piece[...] = (
        BETA_ONE * old + (1.0 - BETA_ONE) * piece.astype(jnp.float32)
    ).astype(jnp.bfloat16)
    g.z_stage(grad_piece)
    s_spread = Spread(
        place,
        copies,
        stat_piece,
        all_stat.at[place.z, quarter(place.p), :],
        local.at[5],
    )
    m.z_stage(moment_piece)

    l.q_third()
    l.p_first()
    r.q_third()
    r.p_first()
    l.p_second()
    r.p_second()
    g.q_first()
    l.p_third()
    r.p_third()
    g.q_second()
    g.q_third()
    g.p_first()
    g.p_second()
    s_spread.arrived()
    s_in.first()
    g.p_third()
    m.q_first()
    s_in.second()
    m.q_second()
    g.finish()
    s_in.arrived()
    renew_stat(place, all_grad, all_stat, new_stat)
    s_out.first()
    m.q_third()
    r.finish()
    own = g.rows(place.p)
    pair = jnp.concatenate(
        [all_grad[:, own, :].reshape(ROWS, ORDER), all_moment[:, own, :].reshape(ROWS, ORDER)]
    )
    right_cols = bases[1, :, :, pl.ds(pl.multiple_of(place.z * ROWS, ROWS), ROWS)]
    turned = jnp.dot(
        pair, right_cols.reshape(ORDER, ROWS), preferred_element_type=jnp.float32
    ).astype(jnp.bfloat16)
    all_turned[:, own, :ROWS] = turned[:ROWS].reshape(SHARDS, height, ROWS)
    all_turned[:, own, ROWS:] = turned[ROWS:].reshape(SHARDS, height, ROWS)
    t.p_first()
    l.finish()
    left_rot, right_rot, rot = bases.at[0], bases.at[1], bases.at[place.core]
    for index in range(SIDE):
        product[:, cols(index)] = quarter_product(place, new_stat, rot, (0,), index)
    t.p_second()
    s_out.second()
    t.p_third()
    for index in range(SIDE):
        product[:, cols(index)] += quarter_product(place, new_stat, rot, (1, 3), index)
    t.finish()
    loads[6].wait()
    rotate(left_rot, all_turned, own_second, out_second, scaled)
    half_rows = pl.ds(pl.multiple_of(place.core * (ROWS // 2), ROWS // 2), ROWS // 2)
    back[...] = (
        multiply(left_rot[:, half_rows, :].reshape(ORDER // 2, ORDER), scaled[...])
        .astype(jnp.bfloat16)
        .reshape(SHARDS, ROWS // 2, ROWS)
    )
    here = pl.ds(pl.multiple_of(place.z * ROWS, ROWS), ROWS)
    back_copies = [
        copies.start(
            back.at[lax.rem(place.z + step, SHARDS)],
            back_rows.at[half_rows, here],
            place.along_z(step),
        )
        for step in (7, 1, 6, 2, 5, 3, 4)
    ]
    back_rows[half_rows, here] = back[place.z]
    s_out.arrived()
    for index in range(SIDE):
        whole = product[:, cols(index)] + quarter_product(place, new_stat, rot, (2,), index)
        current[:, :, cols(index)] = normalize(whole)
    for _ in range(NS_ITERS - 1):
        newton_schulz(current, gram, later)
        current, later = later, current
    for copy in back_copies:
        copy.wait_recv()
    share = back_rows.at[half_rows, :]
    share_copy = copies.start(share, share, place.sibling())
    rows = current[place.z]

    for index in range(SIDE):
        block = contract_cols(rows, rows_of(current, index)) / ORDER
        gram_rows[:, cols(index)] = block.astype(jnp.bfloat16)

    result_copies = []
    for index in range(SIDE):
        span = slice(index * COLS, (index + 1) * COLS)
        out_bases[place.core, :, span] = 1.5 * rows[:, span].astype(jnp.float32) - 0.5 * multiply(
            gram_rows[...], current[:, :, span].reshape(ORDER, COLS)
        )
        block = out_bases.at[place.core, :, span]
        result_copies.append(copies.start(block, block, place.sibling()))

    share_copy.wait_recv()

    for index in range(SIDE):
        block = contract_cols(back_rows[...], rows_of(right_rot, index)) / ORDER
        out_update[:, cols(index)] = block.astype(jnp.bfloat16)

    for copy in result_copies:
        copy.wait_recv()
    copies.finish()


def step(*operands):
    whole = (SHARDS, ROWS, ORDER)
    part = (SHARDS, ROWS, COLS)
    height = ROWS // SIDE // 2
    f32, bf16 = jnp.float32, jnp.bfloat16
    return pl.pallas_call(
        step_kernel,
        out_shape=[
            jax.ShapeDtypeStruct((ROWS, ORDER), bf16),
            jax.ShapeDtypeStruct((ORDER, ROWS), f32),
            jax.ShapeDtypeStruct((2, ROWS, ORDER), f32),
        ],
        in_specs=[pl.BlockSpec(memory_space=pl.ANY)] * 7,
        out_specs=[pl.BlockSpec(memory_space=pltpu.VMEM)] * 3,
        scratch_shapes=[
            pltpu.VMEM((2, *whole), bf16),
            pltpu.VMEM(whole, bf16),
            pltpu.VMEM(whole, bf16),
            pltpu.VMEM(part, bf16),
            pltpu.VMEM(part, f32),
            pltpu.VMEM(whole, bf16),
            pltpu.VMEM(whole, bf16),
            pltpu.VMEM(whole, bf16),
            pltpu.VMEM(whole, bf16),
            pltpu.VMEM((ROWS, ORDER), bf16),
            pltpu.VMEM((ORDER, ROWS), bf16),
            pltpu.VMEM((SHARDS, ROWS // 2, ROWS), bf16),
            pltpu.VMEM((ROWS, ORDER), bf16),
            pltpu.VMEM((ORDER, ORDER), f32),
            pltpu.VMEM((7, height, ORDER), bf16),
            pltpu.VMEM((height, ORDER), f32),
            pltpu.VMEM((SIDE - 1, height, COLS), f32),
            pltpu.VMEM((height, COLS), f32),
            pltpu.VMEM((height, COLS), f32),
            pltpu.VMEM((height, COLS), bf16),
            pltpu.VMEM((height, COLS), bf16),
            pltpu.VMEM((height, ORDER), bf16),
            pltpu.VMEM((ORDER, ROWS), f32),
            pltpu.VMEM((height, COLS), f32),
            pltpu.VMEM((2, 2 * height, COLS), f32),
            pltpu.VMEM((2, height, COLS), f32),
            pltpu.VMEM((2, height, COLS), bf16),
            pltpu.VMEM((2 * height, COLS), f32),
            pltpu.SemaphoreType.DMA((COPIES,)),
            pltpu.SemaphoreType.DMA((COPIES,)),
            pltpu.SemaphoreType.DMA((LOCALS,)),
        ],
        compiler_params=pltpu.CompilerParams(collective_id=0, has_side_effects=True),
        name="step",
    )(*operands)


def deliver_kernel(
    update, second, bases, out_update, out_second, out_left, out_right,
    held_update, held_second, held_bases, sems_in, sems_out,
):
    routes = (
        (bases.at[0], held_bases.at[0], out_left),
        (bases.at[1], held_bases.at[1], out_right),
        (second, held_second, out_second),
        (update, held_update, out_update),
    )
    loads = [
        pltpu.make_async_copy(src, held, sems_in.at[index])
        for index, (src, held, _) in enumerate(routes)
    ]
    stores = [
        pltpu.make_async_copy(held, dst, sems_out.at[index])
        for index, (_, held, dst) in enumerate(routes)
    ]
    for load in loads:
        load.start()
    for load, store in zip(loads, stores):
        load.wait()
        store.start()
    for store in stores:
        store.wait()


def deliver(update, second, bases):
    one = jax.ShapeDtypeStruct(bases.shape[1:], bases.dtype)
    outs = [jax.ShapeDtypeStruct(array.shape, array.dtype) for array in (update, second)]
    return pl.pallas_call(
        deliver_kernel,
        out_shape=[*outs, one, one],
        in_specs=[pl.BlockSpec(memory_space=pl.ANY)] * 3,
        out_specs=[pl.BlockSpec(memory_space=pl.ANY)] * 4,
        scratch_shapes=[
            pltpu.VMEM(update.shape, update.dtype),
            pltpu.VMEM(second.shape, second.dtype),
            pltpu.VMEM(bases.shape, bases.dtype),
            pltpu.SemaphoreType.DMA((4,)),
            pltpu.SemaphoreType.DMA((4,)),
        ],
        name="deliver",
    )(update, second, bases)


def body(group_grads, moment, second, stat_left, stat_right, basis_left, basis_right):
    update, second_new, bases = step(
        group_grads[0], moment, second, stat_left, stat_right, basis_left, basis_right
    )
    return tuple(deliver(update, second_new, bases))


def solution(mesh):
    return jax.shard_map(
        body,
        mesh=mesh,
        in_specs=(
            P("dp", "shard", None),
            P("shard", None),
            P(None, "shard"),
            P("shard", None),
            P("shard", None),
            P("shard", None),
            P("shard", None),
        ),
        out_specs=(P("shard", None), P(None, "shard"), P("shard", None), P("shard", None)),
        check_vma=False,
    )
```

```python
import jax
import jax.numpy as jnp
from jax import lax
from jax.experimental import pallas as pl
from jax.experimental.pallas import tpu as pltpu
from jax.sharding import PartitionSpec as P

NS_ITERS = 2


BETA_ONE = 0.9
BETA_TWO = 0.9
BETA_STAT = 0.95
EPSILON = 1e-08
NORM_EPS = 1e-06

ORDER = 1024
SHARDS = 8
ROWS = ORDER // SHARDS
SIDE = 4
COLS = ORDER // SIDE
COPIES = 120
LOCALS = 13


def contract_rows(left_mat, right_mat):
    return lax.dot_general(
        left_mat, right_mat, (((0,), (0,)), ((), ())), preferred_element_type=jnp.float32
    )


def contract_cols(left_mat, right_mat):
    return lax.dot_general(
        left_mat, right_mat, (((1,), (1,)), ((), ())), preferred_element_type=jnp.float32
    )


class Place:
    def __init__(self):
        data = lax.axis_index("dp")
        self.z = lax.axis_index("shard")
        self.core = lax.rem(data, 2)
        self.zhi = lax.rem(lax.div(data, 2), 2)
        y = lax.rem(lax.div(data, 4), 4)
        x = lax.div(data, 16)
        self.p = x + self.core * (y - x)
        self.q = y + self.core * (x - y)

    def at(self, p, q, zhi, core):
        x = p + self.core * (q - p)
        y = q + self.core * (p - q)
        return ((x * 4 + y) * 2 + zhi) * 2 + core

    def along_p(self, step):
        p = lax.rem(self.p + step, SIDE)
        return (self.at(p, self.q, self.zhi, self.core), self.z)

    def along_q(self, step):
        q = lax.rem(self.q + step, SIDE)
        return (self.at(self.p, q, self.zhi, self.core), self.z)

    def along_z(self, step):
        z = lax.rem(self.z + step, SHARDS)
        return (self.at(self.p, self.q, self.zhi, self.core), z)

    def across_p(self, step):
        p = lax.rem(self.p + step, SIDE)
        return (self.at(p, self.q, self.zhi, 1 - self.core), self.z)

    def across_q(self, step):
        q = lax.rem(self.q + step, SIDE)
        return (self.at(self.p, q, self.zhi, 1 - self.core), self.z)

    def far(self):
        return (self.at(self.p, self.q, 1 - self.zhi, self.core), self.z)

    def sibling(self):
        return (self.at(self.p, self.q, self.zhi, 1 - self.core), self.z)


class Copies:
    def __init__(self, send, recv):
        self.send, self.recv, self.count, self.started = send, recv, 0, []

    def start(self, src, dst, device):
        copy = pltpu.make_async_remote_copy(
            src_ref=src,
            dst_ref=dst,
            send_sem=self.send.at[self.count],
            recv_sem=self.recv.at[self.count],
            device_id=device,
            device_id_type=pl.DeviceIdType.MESH,
        )
        self.count += 1
        copy.start()
        self.started.append(copy)
        return copy

    def finish(self):
        for copy in self.started:
            copy.wait_send()


class Ring:
    def __init__(self, copies, spot, along):
        self.copies, self.spot, self.along = copies, spot, along

    def first(self):
        own = self.spot(0, pl.ds(0, SHARDS))
        self.stage = [
            self.copies.start(own, own, self.along(1)),
            self.copies.start(own, own, self.along(3)),
        ]

    def second(self):
        self.arrived()
        low, high = pl.ds(0, SHARDS // 2), pl.ds(SHARDS // 2, SHARDS // 2)
        self.stage = [
            self.copies.start(self.spot(3, low), self.spot(3, low), self.along(1)),
            self.copies.start(self.spot(1, high), self.spot(1, high), self.along(3)),
        ]

    def arrived(self):
        for copy in self.stage:
            copy.wait_recv()


class Spread:
    def __init__(self, place, copies, piece, spot, local_sem):
        self.local = pltpu.make_async_copy(piece, spot, local_sem)
        self.local.start()
        self.stage = [
            copies.start(piece, spot, place.along_z(step)) for step in (7, 1, 6, 2, 5, 3, 4)
        ]

    def arrived(self):
        self.local.wait()
        for copy in self.stage:
            copy.wait_recv()


class Gather:
    def __init__(self, place, copies, local_sem, out):
        self.place, self.copies, self.local_sem, self.out = place, copies, local_sem, out
        self.q_ring = Ring(copies, self.q_spot, place.along_q)
        self.p_ring = Ring(copies, self.p_spot, place.along_p)
        self.to_core = []

    def rows(self, p):
        height = ROWS // SIDE // 2
        start = self.place.core * (ROWS // 2) + p * height
        return pl.ds(pl.multiple_of(start, height), height)

    def piece(self, ref):
        return ref.at[self.rows(self.place.p), cols(self.place.q)]

    def z_stage(self, piece):
        place = self.place
        spot = self.out.at[place.z, self.rows(place.p), cols(place.q)]
        self.spread = Spread(place, self.copies, piece, spot, self.local_sem)

    def q_spot(self, step, zs):
        q = lax.rem(self.place.q + step, SIDE)
        return self.out.at[zs, self.rows(self.place.p), cols(q)]

    def p_spot(self, step, zs):
        p = lax.rem(self.place.p + step, SIDE)
        return self.out.at[zs, self.rows(p), :]

    def q_first(self):
        self.spread.arrived()
        self.q_ring.first()

    def q_second(self):
        self.q_ring.second()

    def q_third(self):
        self.q_ring.arrived()

    def p_first(self):
        self.p_ring.first()
        self.share(0)

    def p_second(self):
        self.p_ring.second()
        self.share(1)
        self.share(3)

    def p_third(self):
        self.p_ring.arrived()
        self.share(2)

    def finish(self):
        for copy in self.to_core:
            copy.wait_recv()

    def share(self, step):
        block = self.p_spot(step, pl.ds(0, SHARDS))
        self.to_core.append(self.copies.start(block, block, self.place.sibling()))


def cols(q):
    if isinstance(q, int):
        return pl.ds(q * COLS, COLS)
    return pl.ds(pl.multiple_of(q * COLS, COLS), COLS)


def columns_of(ref, index):
    return ref[:, :, cols(index)].reshape(ORDER, COLS)


def rows_of(ref, index):
    return ref[pl.ds(2 * index, 2)].reshape(COLS, ORDER)


def full(ref):
    return ref[...].reshape(ORDER, ORDER)


def multiply(left_mat, right_mat):
    return jnp.dot(left_mat, right_mat, preferred_element_type=jnp.float32)


def rotate(left_rot, turned, second, out_second, scaled):
    for index in range(SIDE):
        rotated = contract_rows(columns_of(left_rot, index), turned[...].reshape(ORDER, COLS))
        rotated = rotated / ORDER
        grad_rot, moment_rot = rotated[:, :ROWS], rotated[:, ROWS:]
        new = BETA_TWO * second[cols(index), :] + (1.0 - BETA_TWO) * grad_rot * grad_rot
        out_second[cols(index), :] = new
        scaled[cols(index), :] = (moment_rot / (jnp.sqrt(new) + EPSILON)).astype(jnp.bfloat16)


def quarter_product(place, stat, rot, steps, index):
    total = None
    for step in steps:
        part = lax.rem(place.q + step, SIDE)
        term = multiply(
            columns_of(stat, part), rot[pl.ds(2 * part, 2), :, cols(index)].reshape(COLS, COLS)
        )
        total = term if total is None else total + term
    return total


def normalize(product):
    squares = jnp.sum(product * product, axis=0, keepdims=True)
    start = product / jnp.sqrt(squares / ORDER + NORM_EPS)
    return start.astype(jnp.bfloat16).reshape(SHARDS, ROWS, COLS)


def newton_schulz(current, gram, later):
    for index in range(SIDE):
        block = contract_cols(full(current), rows_of(current, index)) / ORDER
        gram[:, :, cols(index)] = block.astype(jnp.bfloat16).reshape(SHARDS, ROWS, COLS)

    for index in range(SIDE):
        mine = columns_of(current, index)
        block = 1.5 * mine.astype(jnp.float32) - 0.5 * multiply(full(gram), mine)
        later[:, :, cols(index)] = block.astype(jnp.bfloat16).reshape(SHARDS, ROWS, COLS)


def renew_stat(place, grad, stat, out):
    mine = cols(place.q)

    def keep(pair, outer):
        new = BETA_STAT * stat[pair] + (1.0 - BETA_STAT) * outer.reshape(2, ROWS, COLS)
        out[pair, :, mine] = new.astype(jnp.bfloat16)

    @pl.when(place.core == 0)
    def _():
        other = grad[pl.ds(2 * place.q, 2)].reshape(COLS, ORDER)

        for index in range(SIDE):
            pair = pl.ds(2 * index, 2)
            keep(pair, contract_cols(grad[pair].reshape(COLS, ORDER), other))

    @pl.when(place.core == 1)
    def _():
        other = grad[:, :, mine].reshape(ORDER, COLS)

        for index in range(SIDE):
            block = grad[:, :, cols(index)].reshape(ORDER, COLS)
            keep(pl.ds(2 * index, 2), contract_rows(block, other))


def step_kernel(
    grads, moment, second, stat_left, stat_right, base_left, base_right,
    out_update, out_second, out_bases,
    bases, all_grad, all_moment, all_turned, all_stat, new_stat,
    current, gram, later, gram_rows, scaled, back, back_rows,
    product, recv1, acc1, recv2, acc2, recv3, grad_piece, moment_piece,
    own_grads, own_second, old_moment, stat_pieces, base_pieces, sent_bases, stat_piece,
    send, recv, local,
):
    place = Place()
    height = ROWS // SIDE // 2

    def quarter(p):
        return pl.ds(pl.multiple_of(p * (ROWS // SIDE), ROWS // SIDE), ROWS // SIDE)

    copies = Copies(send, recv)
    g, m, l, r, t = [
        Gather(place, copies, local.at[index], out)
        for index, out in enumerate(
            (all_grad, all_moment, bases.at[0], bases.at[1], all_turned)
        )
    ]
    stat_spot = (quarter(place.p), cols(place.q))
    loads = [
        pltpu.make_async_copy(src, dst, local.at[6 + index])
        for index, (src, dst) in enumerate(
            (
                (l.piece(base_left), base_pieces.at[0]),
                (r.piece(base_right), base_pieces.at[1]),
                (stat_left.at[stat_spot], stat_pieces.at[0]),
                (stat_right.at[stat_spot], stat_pieces.at[1]),
                (grads.at[g.rows(place.p), :], own_grads),
                (g.piece(moment), old_moment),
                (second, own_second),
            )
        )
    ]
    for load in loads:
        load.start()

    for load in loads[:4]:
        load.wait()
    sent_bases[...] = base_pieces[...].astype(jnp.bfloat16)
    stat_piece[...] = stat_pieces[place.core]

    barrier = pltpu.get_barrier_semaphore()
    partners = [place.sibling(), place.far()]
    partners += [place.along_p(step) for step in (1, 2, 3)]
    partners += [place.along_q(step) for step in (1, 2, 3)]
    partners += [place.across_p(step) for step in (1, 2, 3)]
    partners += [place.across_q(step) for step in (1, 2, 3)]
    partners += [place.along_z(step) for step in range(1, SHARDS)]
    for partner in partners:
        pl.semaphore_signal(
            barrier, inc=1, device_id=partner, device_id_type=pl.DeviceIdType.MESH
        )
    pl.semaphore_wait(barrier, len(partners))

    def stat_p_spot(step, zs):
        return all_stat.at[zs, quarter(lax.rem(place.p + step, SIDE)), :]

    def stat_q_spot(step, zs):
        return new_stat.at[zs, :, cols(lax.rem(place.q + step, SIDE))]

    s_in = Ring(copies, stat_p_spot, place.along_p)
    s_out = Ring(copies, stat_q_spot, place.along_q)

    def other_rows(p):
        start = (1 - place.core) * (ROWS // 2) + p * height
        return pl.ds(pl.multiple_of(start, height), height)

    sum_copies = [
        copies.start(
            grads.at[g.rows(lax.rem(place.p + step, SIDE)), :],
            recv1.at[step - 1],
            place.along_p(step),
        )
        for step in (1, 3, 2)
    ]
    sum_copies += [
        copies.start(
            grads.at[other_rows(lax.rem(place.q + step, SIDE)), :],
            recv1.at[3 + step],
            place.across_q(step),
        )
        for step in (0, 1, 3, 2)
    ]
    l.z_stage(sent_bases.at[0])
    r.z_stage(sent_bases.at[1])
    loads[4].wait()
    for copy in sum_copies:
        copy.wait_recv()
    total = own_grads[...].astype(jnp.float32)
    for index in range(7):
        total = total + recv1[index].astype(jnp.float32)
    acc1[...] = total
    q_copies = [
        copies.start(
            acc1.at[:, cols(lax.rem(place.q + step, SIDE))],
            recv2.at[step - 1],
            place.along_q(step),
        )
        for step in (1, 3, 2)
    ]
    for copy in q_copies:
        copy.wait_recv()
    acc2[...] = (acc1[:, cols(place.q)] + recv2[0]) + (recv2[1] + recv2[2])
    far_copy = copies.start(acc2, recv3, place.far())
    l.q_first()
    r.q_first()
    l.q_second()
    r.q_second()
    far_copy.wait_recv()
    piece = (acc2[...] + recv3[...]).astype(jnp.bfloat16)
    grad_piece[...] = piece
    loads[5].wait()
    old = old_moment[...]
    moment_piece[...] = (
        BETA_ONE * old + (1.0 - BETA_ONE) * piece.astype(jnp.float32)
    ).astype(jnp.bfloat16)
    g.z_stage(grad_piece)
    m.z_stage(moment_piece)
    s_spread = Spread(
        place,
        copies,
        stat_piece,
        all_stat.at[place.z, quarter(place.p), :],
        local.at[5],
    )

    l.q_third()
    l.p_first()
    r.q_third()
    r.p_first()
    l.p_second()
    r.p_second()
    g.q_first()
    m.q_first()
    l.p_third()
    r.p_third()
    g.q_second()
    m.q_second()
    g.q_third()
    g.p_first()
    m.q_third()
    r.finish()
    own = g.rows(place.p)
    pair = jnp.concatenate(
        [all_grad[:, own, :].reshape(ROWS, ORDER), all_moment[:, own, :].reshape(ROWS, ORDER)]
    )
    right_cols = bases[1, :, :, pl.ds(pl.multiple_of(place.z * ROWS, ROWS), ROWS)]
    turned = jnp.dot(
        pair, right_cols.reshape(ORDER, ROWS), preferred_element_type=jnp.float32
    ).astype(jnp.bfloat16)
    all_turned[:, own, :ROWS] = turned[:ROWS].reshape(SHARDS, height, ROWS)
    all_turned[:, own, ROWS:] = turned[ROWS:].reshape(SHARDS, height, ROWS)
    t.p_first()
    g.p_second()
    s_spread.arrived()
    s_in.first()
    t.p_second()
    g.p_third()
    s_in.second()
    t.p_third()
    g.finish()
    s_in.arrived()
    renew_stat(place, all_grad, all_stat, new_stat)
    s_out.first()
    l.finish()
    t.finish()
    loads[6].wait()
    left_rot, right_rot, rot = bases.at[0], bases.at[1], bases.at[place.core]
    rotate(left_rot, all_turned, own_second, out_second, scaled)
    half_rows = pl.ds(pl.multiple_of(place.core * (ROWS // 2), ROWS // 2), ROWS // 2)
    back[...] = (
        multiply(left_rot[:, half_rows, :].reshape(ORDER // 2, ORDER), scaled[...])
        .astype(jnp.bfloat16)
        .reshape(SHARDS, ROWS // 2, ROWS)
    )
    here = pl.ds(pl.multiple_of(place.z * ROWS, ROWS), ROWS)
    back_copies = [
        copies.start(
            back.at[lax.rem(place.z + step, SHARDS)],
            back_rows.at[half_rows, here],
            place.along_z(step),
        )
        for step in (7, 1, 6, 2, 5, 3, 4)
    ]
    back_rows[half_rows, here] = back[place.z]
    for index in range(SIDE):
        product[:, cols(index)] = quarter_product(place, new_stat, rot, (0,), index)
    s_out.second()
    for index in range(SIDE):
        product[:, cols(index)] += quarter_product(place, new_stat, rot, (1, 3), index)
    s_out.arrived()
    for index in range(SIDE):
        whole = product[:, cols(index)] + quarter_product(place, new_stat, rot, (2,), index)
        current[:, :, cols(index)] = normalize(whole)
    for _ in range(NS_ITERS - 1):
        newton_schulz(current, gram, later)
        current, later = later, current
    for copy in back_copies:
        copy.wait_recv()
    share = back_rows.at[half_rows, :]
    share_copy = copies.start(share, share, place.sibling())
    rows = current[place.z]

    for index in range(SIDE):
        block = contract_cols(rows, rows_of(current, index)) / ORDER
        gram_rows[:, cols(index)] = block.astype(jnp.bfloat16)

    result_copies = []
    for index in range(SIDE):
        span = slice(index * COLS, (index + 1) * COLS)
        out_bases[place.core, :, span] = 1.5 * rows[:, span].astype(jnp.float32) - 0.5 * multiply(
            gram_rows[...], current[:, :, span].reshape(ORDER, COLS)
        )
        block = out_bases.at[place.core, :, span]
        result_copies.append(copies.start(block, block, place.sibling()))

    share_copy.wait_recv()

    for index in range(SIDE):
        block = contract_cols(back_rows[...], rows_of(right_rot, index)) / ORDER
        out_update[:, cols(index)] = block.astype(jnp.bfloat16)

    for copy in result_copies:
        copy.wait_recv()
    copies.finish()


def step(*operands):
    whole = (SHARDS, ROWS, ORDER)
    part = (SHARDS, ROWS, COLS)
    height = ROWS // SIDE // 2
    f32, bf16 = jnp.float32, jnp.bfloat16
    return pl.pallas_call(
        step_kernel,
        out_shape=[
            jax.ShapeDtypeStruct((ROWS, ORDER), bf16),
            jax.ShapeDtypeStruct((ORDER, ROWS), f32),
            jax.ShapeDtypeStruct((2, ROWS, ORDER), f32),
        ],
        in_specs=[pl.BlockSpec(memory_space=pl.ANY)] * 7,
        out_specs=[pl.BlockSpec(memory_space=pltpu.VMEM)] * 3,
        scratch_shapes=[
            pltpu.VMEM((2, *whole), bf16),
            pltpu.VMEM(whole, bf16),
            pltpu.VMEM(whole, bf16),
            pltpu.VMEM(part, bf16),
            pltpu.VMEM(part, f32),
            pltpu.VMEM(whole, bf16),
            pltpu.VMEM(whole, bf16),
            pltpu.VMEM(whole, bf16),
            pltpu.VMEM(whole, bf16),
            pltpu.VMEM((ROWS, ORDER), bf16),
            pltpu.VMEM((ORDER, ROWS), bf16),
            pltpu.VMEM((SHARDS, ROWS // 2, ROWS), bf16),
            pltpu.VMEM((ROWS, ORDER), bf16),
            pltpu.VMEM((ORDER, ORDER), f32),
            pltpu.VMEM((7, height, ORDER), bf16),
            pltpu.VMEM((height, ORDER), f32),
            pltpu.VMEM((SIDE - 1, height, COLS), f32),
            pltpu.VMEM((height, COLS), f32),
            pltpu.VMEM((height, COLS), f32),
            pltpu.VMEM((height, COLS), bf16),
            pltpu.VMEM((height, COLS), bf16),
            pltpu.VMEM((height, ORDER), bf16),
            pltpu.VMEM((ORDER, ROWS), f32),
            pltpu.VMEM((height, COLS), f32),
            pltpu.VMEM((2, 2 * height, COLS), f32),
            pltpu.VMEM((2, height, COLS), f32),
            pltpu.VMEM((2, height, COLS), bf16),
            pltpu.VMEM((2 * height, COLS), f32),
            pltpu.SemaphoreType.DMA((COPIES,)),
            pltpu.SemaphoreType.DMA((COPIES,)),
            pltpu.SemaphoreType.DMA((LOCALS,)),
        ],
        compiler_params=pltpu.CompilerParams(collective_id=0, has_side_effects=True),
        name="step",
    )(*operands)


def deliver_kernel(
    update, second, bases, out_update, out_second, out_left, out_right,
    held_update, held_second, held_bases, sems_in, sems_out,
):
    routes = (
        (bases.at[0], held_bases.at[0], out_left),
        (bases.at[1], held_bases.at[1], out_right),
        (second, held_second, out_second),
        (update, held_update, out_update),
    )
    loads = [
        pltpu.make_async_copy(src, held, sems_in.at[index])
        for index, (src, held, _) in enumerate(routes)
    ]
    stores = [
        pltpu.make_async_copy(held, dst, sems_out.at[index])
        for index, (_, held, dst) in enumerate(routes)
    ]
    for load in loads:
        load.start()
    for load, store in zip(loads, stores):
        load.wait()
        store.start()
    for store in stores:
        store.wait()


def deliver(update, second, bases):
    one = jax.ShapeDtypeStruct(bases.shape[1:], bases.dtype)
    outs = [jax.ShapeDtypeStruct(array.shape, array.dtype) for array in (update, second)]
    return pl.pallas_call(
        deliver_kernel,
        out_shape=[*outs, one, one],
        in_specs=[pl.BlockSpec(memory_space=pl.ANY)] * 3,
        out_specs=[pl.BlockSpec(memory_space=pl.ANY)] * 4,
        scratch_shapes=[
            pltpu.VMEM(update.shape, update.dtype),
            pltpu.VMEM(second.shape, second.dtype),
            pltpu.VMEM(bases.shape, bases.dtype),
            pltpu.SemaphoreType.DMA((4,)),
            pltpu.SemaphoreType.DMA((4,)),
        ],
        name="deliver",
    )(update, second, bases)


def body(group_grads, moment, second, stat_left, stat_right, basis_left, basis_right):
    update, second_new, bases = step(
        group_grads[0], moment, second, stat_left, stat_right, basis_left, basis_right
    )
    return tuple(deliver(update, second_new, bases))


def solution(mesh):
    return jax.shard_map(
        body,
        mesh=mesh,
        in_specs=(
            P("dp", "shard", None),
            P("shard", None),
            P(None, "shard"),
            P("shard", None),
            P("shard", None),
            P("shard", None),
            P("shard", None),
        ),
        out_specs=(P("shard", None), P(None, "shard"), P("shard", None), P("shard", None)),
        check_vma=False,
    )
```

```python
import jax
import jax.numpy as jnp
from jax import lax
from jax.experimental import pallas as pl
from jax.experimental.pallas import tpu as pltpu
from jax.sharding import PartitionSpec as P

NS_ITERS = 2


BETA_ONE = 0.9
BETA_TWO = 0.9
BETA_STAT = 0.95
EPSILON = 1e-08
NORM_EPS = 1e-06

ORDER = 1024
SHARDS = 8
ROWS = ORDER // SHARDS
SIDE = 4
COLS = ORDER // SIDE
COPIES = 150
LOCALS = 13


def contract_rows(left_mat, right_mat):
    return lax.dot_general(
        left_mat, right_mat, (((0,), (0,)), ((), ())), preferred_element_type=jnp.float32
    )


def contract_cols(left_mat, right_mat):
    return lax.dot_general(
        left_mat, right_mat, (((1,), (1,)), ((), ())), preferred_element_type=jnp.float32
    )


class Place:
    def __init__(self):
        data = lax.axis_index("dp")
        self.z = lax.axis_index("shard")
        self.core = lax.rem(data, 2)
        self.zhi = lax.rem(lax.div(data, 2), 2)
        y = lax.rem(lax.div(data, 4), 4)
        x = lax.div(data, 16)
        self.p = x + self.core * (y - x)
        self.q = y + self.core * (x - y)

    def at(self, p, q, zhi, core):
        x = p + self.core * (q - p)
        y = q + self.core * (p - q)
        return ((x * 4 + y) * 2 + zhi) * 2 + core

    def along_p(self, step):
        p = lax.rem(self.p + step, SIDE)
        return (self.at(p, self.q, self.zhi, self.core), self.z)

    def along_q(self, step):
        q = lax.rem(self.q + step, SIDE)
        return (self.at(self.p, q, self.zhi, self.core), self.z)

    def along_z(self, step):
        z = lax.rem(self.z + step, SHARDS)
        return (self.at(self.p, self.q, self.zhi, self.core), z)

    def across_p(self, step):
        p = lax.rem(self.p + step, SIDE)
        return (self.at(p, self.q, self.zhi, 1 - self.core), self.z)

    def across_q(self, step):
        q = lax.rem(self.q + step, SIDE)
        return (self.at(self.p, q, self.zhi, 1 - self.core), self.z)

    def far(self):
        return (self.at(self.p, self.q, 1 - self.zhi, self.core), self.z)

    def sibling(self):
        return (self.at(self.p, self.q, self.zhi, 1 - self.core), self.z)


class Copies:
    def __init__(self, send, recv):
        self.send, self.recv, self.count, self.started = send, recv, 0, []

    def start(self, src, dst, device):
        copy = pltpu.make_async_remote_copy(
            src_ref=src,
            dst_ref=dst,
            send_sem=self.send.at[self.count],
            recv_sem=self.recv.at[self.count],
            device_id=device,
            device_id_type=pl.DeviceIdType.MESH,
        )
        self.count += 1
        copy.start()
        self.started.append(copy)
        return copy

    def finish(self):
        for copy in self.started:
            copy.wait_send()


class Ring:
    def __init__(self, copies, spot, along):
        self.copies, self.spot, self.along = copies, spot, along

    def send(self, step, zs, to):
        part = self.spot(step, zs)
        return self.copies.start(part, part, self.along(to))

    def first(self):
        low, high = pl.ds(0, SHARDS // 2), pl.ds(SHARDS // 2, SHARDS // 2)
        self.early = [self.send(0, low, 1), self.send(0, high, 3)]
        self.late = [self.send(0, high, 1), self.send(0, low, 3)]

    def second(self):
        low, high = pl.ds(0, SHARDS // 2), pl.ds(SHARDS // 2, SHARDS // 2)
        for copy in self.early:
            copy.wait_recv()
        self.last = [self.send(3, low, 1), self.send(1, high, 3)]

    def near(self):
        for copy in self.late:
            copy.wait_recv()
        self.late = []

    def arrived(self):
        self.near()
        for copy in self.last:
            copy.wait_recv()


class Spread:
    def __init__(self, place, copies, piece, spot, local_sem):
        self.local = pltpu.make_async_copy(piece, spot, local_sem)
        self.local.start()
        self.stage = [
            copies.start(piece, spot, place.along_z(step)) for step in (7, 1, 6, 2, 5, 3, 4)
        ]

    def arrived(self):
        self.local.wait()
        for copy in self.stage:
            copy.wait_recv()


class Gather:
    def __init__(self, place, copies, local_sem, out):
        self.place, self.copies, self.local_sem, self.out = place, copies, local_sem, out
        self.q_ring = Ring(copies, self.q_spot, place.along_q)
        self.p_ring = Ring(copies, self.p_spot, place.along_p)
        self.to_core = []

    def rows(self, p):
        height = ROWS // SIDE // 2
        start = self.place.core * (ROWS // 2) + p * height
        return pl.ds(pl.multiple_of(start, height), height)

    def piece(self, ref):
        return ref.at[self.rows(self.place.p), cols(self.place.q)]

    def z_stage(self, piece):
        place = self.place
        spot = self.out.at[place.z, self.rows(place.p), cols(place.q)]
        self.spread = Spread(place, self.copies, piece, spot, self.local_sem)

    def q_spot(self, step, zs):
        q = lax.rem(self.place.q + step, SIDE)
        return self.out.at[zs, self.rows(self.place.p), cols(q)]

    def p_spot(self, step, zs):
        p = lax.rem(self.place.p + step, SIDE)
        return self.out.at[zs, self.rows(p), :]

    def q_first(self):
        self.spread.arrived()
        self.q_ring.first()

    def q_second(self):
        self.q_ring.second()

    def q_third(self):
        self.q_ring.arrived()

    def p_first(self):
        self.p_ring.first()
        self.share(0)

    def p_second(self):
        self.p_ring.second()
        self.p_ring.near()
        self.share(1)
        self.share(3)

    def p_third(self):
        self.p_ring.arrived()
        self.share(2)

    def finish(self):
        for copy in self.to_core:
            copy.wait_recv()

    def share(self, step):
        block = self.p_spot(step, pl.ds(0, SHARDS))
        self.to_core.append(self.copies.start(block, block, self.place.sibling()))


def cols(q):
    if isinstance(q, int):
        return pl.ds(q * COLS, COLS)
    return pl.ds(pl.multiple_of(q * COLS, COLS), COLS)


def columns_of(ref, index):
    return ref[:, :, cols(index)].reshape(ORDER, COLS)


def rows_of(ref, index):
    return ref[pl.ds(2 * index, 2)].reshape(COLS, ORDER)


def full(ref):
    return ref[...].reshape(ORDER, ORDER)


def multiply(left_mat, right_mat):
    return jnp.dot(left_mat, right_mat, preferred_element_type=jnp.float32)


def rotate(left_rot, turned, second, out_second, scaled):
    for index in range(SIDE):
        rotated = contract_rows(columns_of(left_rot, index), turned[...].reshape(ORDER, COLS))
        rotated = rotated / ORDER
        grad_rot, moment_rot = rotated[:, :ROWS], rotated[:, ROWS:]
        new = BETA_TWO * second[cols(index), :] + (1.0 - BETA_TWO) * grad_rot * grad_rot
        out_second[cols(index), :] = new
        scaled[cols(index), :] = (moment_rot / (jnp.sqrt(new) + EPSILON)).astype(jnp.bfloat16)


def quarter_product(place, stat, rot, steps, index):
    total = None
    for step in steps:
        part = lax.rem(place.q + step, SIDE)
        term = multiply(
            columns_of(stat, part), rot[pl.ds(2 * part, 2), :, cols(index)].reshape(COLS, COLS)
        )
        total = term if total is None else total + term
    return total


def normalize(product):
    squares = jnp.sum(product * product, axis=0, keepdims=True)
    start = product / jnp.sqrt(squares / ORDER + NORM_EPS)
    return start.astype(jnp.bfloat16).reshape(SHARDS, ROWS, COLS)


def newton_schulz(current, gram, later):
    for index in range(SIDE):
        block = contract_cols(full(current), rows_of(current, index)) / ORDER
        gram[:, :, cols(index)] = block.astype(jnp.bfloat16).reshape(SHARDS, ROWS, COLS)

    for index in range(SIDE):
        mine = columns_of(current, index)
        block = 1.5 * mine.astype(jnp.float32) - 0.5 * multiply(full(gram), mine)
        later[:, :, cols(index)] = block.astype(jnp.bfloat16).reshape(SHARDS, ROWS, COLS)


def renew_stat(place, grad, stat, out):
    mine = cols(place.q)

    def keep(pair, outer):
        new = BETA_STAT * stat[pair] + (1.0 - BETA_STAT) * outer.reshape(2, ROWS, COLS)
        out[pair, :, mine] = new.astype(jnp.bfloat16)

    @pl.when(place.core == 0)
    def _():
        other = grad[pl.ds(2 * place.q, 2)].reshape(COLS, ORDER)

        for index in range(SIDE):
            pair = pl.ds(2 * index, 2)
            keep(pair, contract_cols(grad[pair].reshape(COLS, ORDER), other))

    @pl.when(place.core == 1)
    def _():
        other = grad[:, :, mine].reshape(ORDER, COLS)

        for index in range(SIDE):
            block = grad[:, :, cols(index)].reshape(ORDER, COLS)
            keep(pl.ds(2 * index, 2), contract_rows(block, other))


def step_kernel(
    grads, moment, second, stat_left, stat_right, base_left, base_right,
    out_update, out_second, out_bases,
    bases, all_grad, all_moment, all_turned, all_stat, new_stat,
    current, gram, later, gram_rows, scaled, back, back_rows,
    product, recv1, acc1, recv2, acc2, recv3, grad_piece, moment_piece,
    own_grads, own_second, old_moment, stat_pieces, base_pieces, sent_bases, stat_piece,
    send, recv, local,
):
    place = Place()
    height = ROWS // SIDE // 2

    def quarter(p):
        return pl.ds(pl.multiple_of(p * (ROWS // SIDE), ROWS // SIDE), ROWS // SIDE)

    copies = Copies(send, recv)
    g, m, l, r, t = [
        Gather(place, copies, local.at[index], out)
        for index, out in enumerate(
            (all_grad, all_moment, bases.at[0], bases.at[1], all_turned)
        )
    ]
    stat_spot = (quarter(place.p), cols(place.q))
    loads = [
        pltpu.make_async_copy(src, dst, local.at[6 + index])
        for index, (src, dst) in enumerate(
            (
                (l.piece(base_left), base_pieces.at[0]),
                (r.piece(base_right), base_pieces.at[1]),
                (stat_left.at[stat_spot], stat_pieces.at[0]),
                (stat_right.at[stat_spot], stat_pieces.at[1]),
                (grads.at[g.rows(place.p), :], own_grads),
                (g.piece(moment), old_moment),
                (second, own_second),
            )
        )
    ]
    for load in loads:
        load.start()

    for load in loads[:4]:
        load.wait()
    sent_bases[...] = base_pieces[...].astype(jnp.bfloat16)
    stat_piece[...] = stat_pieces[place.core]

    barrier = pltpu.get_barrier_semaphore()
    partners = [place.sibling(), place.far()]
    partners += [place.along_p(step) for step in (1, 2, 3)]
    partners += [place.along_q(step) for step in (1, 2, 3)]
    partners += [place.across_p(step) for step in (1, 2, 3)]
    partners += [place.across_q(step) for step in (1, 2, 3)]
    partners += [place.along_z(step) for step in range(1, SHARDS)]
    for partner in partners:
        pl.semaphore_signal(
            barrier, inc=1, device_id=partner, device_id_type=pl.DeviceIdType.MESH
        )
    pl.semaphore_wait(barrier, len(partners))

    def stat_p_spot(step, zs):
        return all_stat.at[zs, quarter(lax.rem(place.p + step, SIDE)), :]

    def stat_q_spot(step, zs):
        return new_stat.at[zs, :, cols(lax.rem(place.q + step, SIDE))]

    s_in = Ring(copies, stat_p_spot, place.along_p)
    s_out = Ring(copies, stat_q_spot, place.along_q)

    def other_rows(p):
        start = (1 - place.core) * (ROWS // 2) + p * height
        return pl.ds(pl.multiple_of(start, height), height)

    sum_copies = [
        copies.start(
            grads.at[g.rows(lax.rem(place.p + step, SIDE)), :],
            recv1.at[step - 1],
            place.along_p(step),
        )
        for step in (1, 3, 2)
    ]
    sum_copies += [
        copies.start(
            grads.at[other_rows(lax.rem(place.q + step, SIDE)), :],
            recv1.at[3 + step],
            place.across_q(step),
        )
        for step in (0, 1, 3, 2)
    ]
    l.z_stage(sent_bases.at[0])
    r.z_stage(sent_bases.at[1])
    loads[4].wait()
    for copy in sum_copies:
        copy.wait_recv()
    total = own_grads[...].astype(jnp.float32)
    for index in range(7):
        total = total + recv1[index].astype(jnp.float32)
    acc1[...] = total
    q_copies = [
        copies.start(
            acc1.at[:, cols(lax.rem(place.q + step, SIDE))],
            recv2.at[step - 1],
            place.along_q(step),
        )
        for step in (1, 3, 2)
    ]
    for copy in q_copies:
        copy.wait_recv()
    acc2[...] = (acc1[:, cols(place.q)] + recv2[0]) + (recv2[1] + recv2[2])
    far_copy = copies.start(acc2, recv3, place.far())
    l.q_first()
    r.q_first()
    l.q_second()
    r.q_second()
    far_copy.wait_recv()
    piece = (acc2[...] + recv3[...]).astype(jnp.bfloat16)
    grad_piece[...] = piece
    loads[5].wait()
    old = old_moment[...]
    moment_piece[...] = (
        BETA_ONE * old + (1.0 - BETA_ONE) * piece.astype(jnp.float32)
    ).astype(jnp.bfloat16)
    g.z_stage(grad_piece)
    m.z_stage(moment_piece)
    s_spread = Spread(
        place,
        copies,
        stat_piece,
        all_stat.at[place.z, quarter(place.p), :],
        local.at[5],
    )

    l.q_third()
    l.p_first()
    r.q_third()
    r.p_first()
    l.p_second()
    r.p_second()
    g.q_first()
    m.q_first()
    l.p_third()
    r.p_third()
    g.q_second()
    m.q_second()
    g.q_third()
    g.p_first()
    m.q_third()
    r.finish()
    own = g.rows(place.p)
    pair = jnp.concatenate(
        [all_grad[:, own, :].reshape(ROWS, ORDER), all_moment[:, own, :].reshape(ROWS, ORDER)]
    )
    right_cols = bases[1, :, :, pl.ds(pl.multiple_of(place.z * ROWS, ROWS), ROWS)]
    turned = jnp.dot(
        pair, right_cols.reshape(ORDER, ROWS), preferred_element_type=jnp.float32
    ).astype(jnp.bfloat16)
    all_turned[:, own, :ROWS] = turned[:ROWS].reshape(SHARDS, height, ROWS)
    all_turned[:, own, ROWS:] = turned[ROWS:].reshape(SHARDS, height, ROWS)
    t.p_first()
    g.p_second()
    s_spread.arrived()
    s_in.first()
    t.p_second()
    g.p_third()
    s_in.second()
    t.p_third()
    g.finish()
    s_in.arrived()
    renew_stat(place, all_grad, all_stat, new_stat)
    s_out.first()
    l.finish()
    t.finish()
    loads[6].wait()
    left_rot, right_rot, rot = bases.at[0], bases.at[1], bases.at[place.core]
    rotate(left_rot, all_turned, own_second, out_second, scaled)
    half_rows = pl.ds(pl.multiple_of(place.core * (ROWS // 2), ROWS // 2), ROWS // 2)
    back[...] = (
        multiply(left_rot[:, half_rows, :].reshape(ORDER // 2, ORDER), scaled[...])
        .astype(jnp.bfloat16)
        .reshape(SHARDS, ROWS // 2, ROWS)
    )
    here = pl.ds(pl.multiple_of(place.z * ROWS, ROWS), ROWS)
    back_copies = [
        copies.start(
            back.at[lax.rem(place.z + step, SHARDS)],
            back_rows.at[half_rows, here],
            place.along_z(step),
        )
        for step in (7, 1, 6, 2, 5, 3, 4)
    ]
    back_rows[half_rows, here] = back[place.z]
    for index in range(SIDE):
        product[:, cols(index)] = quarter_product(place, new_stat, rot, (0,), index)
    s_out.second()
    s_out.near()
    for index in range(SIDE):
        product[:, cols(index)] += quarter_product(place, new_stat, rot, (1, 3), index)
    s_out.arrived()
    for index in range(SIDE):
        whole = product[:, cols(index)] + quarter_product(place, new_stat, rot, (2,), index)
        current[:, :, cols(index)] = normalize(whole)
    for _ in range(NS_ITERS - 1):
        newton_schulz(current, gram, later)
        current, later = later, current
    for copy in back_copies:
        copy.wait_recv()
    share = back_rows.at[half_rows, :]
    share_copy = copies.start(share, share, place.sibling())
    rows = current[place.z]

    for index in range(SIDE):
        block = contract_cols(rows, rows_of(current, index)) / ORDER
        gram_rows[:, cols(index)] = block.astype(jnp.bfloat16)

    result_copies = []
    for index in range(SIDE):
        span = slice(index * COLS, (index + 1) * COLS)
        out_bases[place.core, :, span] = 1.5 * rows[:, span].astype(jnp.float32) - 0.5 * multiply(
            gram_rows[...], current[:, :, span].reshape(ORDER, COLS)
        )
        block = out_bases.at[place.core, :, span]
        result_copies.append(copies.start(block, block, place.sibling()))

    share_copy.wait_recv()

    for index in range(SIDE):
        block = contract_cols(back_rows[...], rows_of(right_rot, index)) / ORDER
        out_update[:, cols(index)] = block.astype(jnp.bfloat16)

    for copy in result_copies:
        copy.wait_recv()
    copies.finish()


def step(*operands):
    whole = (SHARDS, ROWS, ORDER)
    part = (SHARDS, ROWS, COLS)
    height = ROWS // SIDE // 2
    f32, bf16 = jnp.float32, jnp.bfloat16
    return pl.pallas_call(
        step_kernel,
        out_shape=[
            jax.ShapeDtypeStruct((ROWS, ORDER), bf16),
            jax.ShapeDtypeStruct((ORDER, ROWS), f32),
            jax.ShapeDtypeStruct((2, ROWS, ORDER), f32),
        ],
        in_specs=[pl.BlockSpec(memory_space=pl.ANY)] * 7,
        out_specs=[pl.BlockSpec(memory_space=pltpu.VMEM)] * 3,
        scratch_shapes=[
            pltpu.VMEM((2, *whole), bf16),
            pltpu.VMEM(whole, bf16),
            pltpu.VMEM(whole, bf16),
            pltpu.VMEM(part, bf16),
            pltpu.VMEM(part, f32),
            pltpu.VMEM(whole, bf16),
            pltpu.VMEM(whole, bf16),
            pltpu.VMEM(whole, bf16),
            pltpu.VMEM(whole, bf16),
            pltpu.VMEM((ROWS, ORDER), bf16),
            pltpu.VMEM((ORDER, ROWS), bf16),
            pltpu.VMEM((SHARDS, ROWS // 2, ROWS), bf16),
            pltpu.VMEM((ROWS, ORDER), bf16),
            pltpu.VMEM((ORDER, ORDER), f32),
            pltpu.VMEM((7, height, ORDER), bf16),
            pltpu.VMEM((height, ORDER), f32),
            pltpu.VMEM((SIDE - 1, height, COLS), f32),
            pltpu.VMEM((height, COLS), f32),
            pltpu.VMEM((height, COLS), f32),
            pltpu.VMEM((height, COLS), bf16),
            pltpu.VMEM((height, COLS), bf16),
            pltpu.VMEM((height, ORDER), bf16),
            pltpu.VMEM((ORDER, ROWS), f32),
            pltpu.VMEM((height, COLS), f32),
            pltpu.VMEM((2, 2 * height, COLS), f32),
            pltpu.VMEM((2, height, COLS), f32),
            pltpu.VMEM((2, height, COLS), bf16),
            pltpu.VMEM((2 * height, COLS), f32),
            pltpu.SemaphoreType.DMA((COPIES,)),
            pltpu.SemaphoreType.DMA((COPIES,)),
            pltpu.SemaphoreType.DMA((LOCALS,)),
        ],
        compiler_params=pltpu.CompilerParams(collective_id=0, has_side_effects=True),
        name="step",
    )(*operands)


def deliver_kernel(
    update, second, bases, out_update, out_second, out_left, out_right,
    held_update, held_second, held_bases, sems_in, sems_out,
):
    routes = (
        (bases.at[0], held_bases.at[0], out_left),
        (bases.at[1], held_bases.at[1], out_right),
        (second, held_second, out_second),
        (update, held_update, out_update),
    )
    loads = [
        pltpu.make_async_copy(src, held, sems_in.at[index])
        for index, (src, held, _) in enumerate(routes)
    ]
    stores = [
        pltpu.make_async_copy(held, dst, sems_out.at[index])
        for index, (_, held, dst) in enumerate(routes)
    ]
    for load in loads:
        load.start()
    for load, store in zip(loads, stores):
        load.wait()
        store.start()
    for store in stores:
        store.wait()


def deliver(update, second, bases):
    one = jax.ShapeDtypeStruct(bases.shape[1:], bases.dtype)
    outs = [jax.ShapeDtypeStruct(array.shape, array.dtype) for array in (update, second)]
    return pl.pallas_call(
        deliver_kernel,
        out_shape=[*outs, one, one],
        in_specs=[pl.BlockSpec(memory_space=pl.ANY)] * 3,
        out_specs=[pl.BlockSpec(memory_space=pl.ANY)] * 4,
        scratch_shapes=[
            pltpu.VMEM(update.shape, update.dtype),
            pltpu.VMEM(second.shape, second.dtype),
            pltpu.VMEM(bases.shape, bases.dtype),
            pltpu.SemaphoreType.DMA((4,)),
            pltpu.SemaphoreType.DMA((4,)),
        ],
        name="deliver",
    )(update, second, bases)


def body(group_grads, moment, second, stat_left, stat_right, basis_left, basis_right):
    update, second_new, bases = step(
        group_grads[0], moment, second, stat_left, stat_right, basis_left, basis_right
    )
    return tuple(deliver(update, second_new, bases))


def solution(mesh):
    return jax.shard_map(
        body,
        mesh=mesh,
        in_specs=(
            P("dp", "shard", None),
            P("shard", None),
            P(None, "shard"),
            P("shard", None),
            P("shard", None),
            P("shard", None),
            P("shard", None),
        ),
        out_specs=(P("shard", None), P(None, "shard"), P("shard", None), P("shard", None)),
        check_vma=False,
    )
```
